32 devices in a mesh: row: 16 (over z, y, x), col: 2 (over core).
Axes of the slice: x: 2, y: 2, z: 4, core: 2. Of those that a mesh axis runs over, the one named last changes fastest.
Arguments:
- vectors_in: bfloat16 [32768, 2048], P('row', 'col'), may hold values from -6 to 6
- panel: bfloat16 [32768, 256], P('row', 'col'), may hold values from -0.03125 to 0.03125
- factor: float32 [256, 256], replicated, may hold values from -3 to 8, as said below
- atom_basis: int32 [16, 128], P('row'), may hold values from 1 to 24, 2048 in all within a row
- proj_count: int32 [2048], P('row'), may hold values from 1 to 16
- coupling: bfloat16 [2048, 9, 384], P('row'), may hold values from -0.4375 to 0.4375
- block_present: int32 [2048, 9], P('row'), may hold values 0 or 1
- occ_mask: int32 [2048], P('col'), may hold values 0 or 1
- occ_weight: float32 [2048], P('col'), may hold values from 0.5 to 2
Outputs:
- vectors: bfloat16 [32768, 2048], P('row', 'col')
- density: float32 [2048, 256], P(('row', 'col'))
The draws below stay inside these ranges and needn't reach their ends.
Inputs may be any that keep to these rules, and one draw needn't show every extreme that they name: `factor`: zero below the diagonal; the diagonal lies in 4 to 8. `atom_basis`: each row sums to 2048, and 24 is reached in each row.
All inputs are finite; a program needn't handle non-finite values. No bound on the sum of `block_present` or of `occ_mask` on one device may be relied on, other than what follows from the above.
Results may differ from the reference program's by a relative error of at most 0.0075.
Values may be sent and summed in bfloat16 or wider, within the bound.
A program may use at most 192 MiB of HBM per device.

```python
import math
import jax
import jax.numpy as jnp
import numpy as np
from jax import lax

M_DEV = 2048
NB_DEV = 1024
NPAN = 256
NPMAX = 16
BMAX = 24
K = 9
A_DEV = 128
M = 32768
NB = 2048
ATOMS = 2048
N_ROW = 16
N_COL = 2


def draw_factor(key, part):
    key_upper, key_diagonal = jax.random.split(key, 2)
    upper = jnp.clip(jax.random.normal(key_upper, (NPAN, NPAN), jnp.float32), -6.0, 6.0) * 0.5
    diagonal = jax.random.uniform(key_diagonal, (NPAN,), jnp.float32, 4.0, 8.0)
    return jnp.triu(upper, 1) + jnp.diag(diagonal)


def place_ends(values, rng, least, high):
    longest = values.shape.index(max(values.shape))
    spots = []
    for shift in (0, 1):
        where = [jax.random.randint(jax.random.fold_in(rng, axis), (), 0, length) for axis, length in enumerate(values.shape)]
        where[longest] = (where[longest] + shift) % values.shape[longest]
        spots.append(tuple(where))
    return values.at[spots[0]].set(least).at[spots[1]].set(high)


def steps_of(key, dims, cuts, smallest, high):
    level, own = 1.0, jax.random.fold_in(key, 6)
    for axis_at, parts in cuts:
        draws = jnp.exp(jax.random.uniform(jax.random.fold_in(own, axis_at), (parts,), jnp.float32, smallest / len(cuts), high / len(cuts)))
        level = level * jnp.repeat(draws, dims[axis_at] // parts).reshape([-1 if axis == axis_at else 1 for axis in range(len(dims))])
    return level


def split_up(number_of, total, most, skew):
    weights = [(1 << 20) // math.isqrt(rank ** skew) + 1 for rank in range(2, number_of + 1)]
    spare, holding = total - most - (number_of - 1), [1] * (number_of - 1)
    while spare > 0:
        candidates = [i for i in range(number_of - 1) if holding[i] < most]
        mass, left = sum([weights[i] for i in candidates]), spare
        for i in candidates:
            extra = min(most - holding[i], max(1, left * weights[i] // mass), spare)
            holding[i] = holding[i] + extra
            spare = spare - extra
    return np.array([most] + holding)


def ragged(rng, amount, total, limit, skew):
    if amount == 2:
        one = jax.random.randint(rng, (), max(1, total - limit), min(limit, total - 1) + 1)
        return jnp.stack([one, total - one])
    tallies = jnp.asarray(split_up(amount, total, limit, skew), jnp.int32)
    pairs = (amount - 1) // 2
    source_of, receiver = tallies[1:1 + 2 * pairs:2], tallies[2:2 + 2 * pairs:2]
    slack = jnp.minimum(source_of - 1, limit - receiver)
    moved = jax.random.randint(jax.random.fold_in(rng, 1), (pairs,), 0, 1 << 20) % (slack + 1)
    tallies = tallies.at[1:1 + 2 * pairs:2].set(source_of - moved).at[2:2 + 2 * pairs:2].set(receiver + moved)
    return tallies[jax.random.permutation(jax.random.fold_in(rng, 2), amount)]


def bell_draw(rng, extent, width, reach, cuts=(), held_as=jnp.bfloat16):
    array = jax.random.normal(rng, extent, jnp.float32) * width
    if len(cuts) > 0:
        array = steps_of(rng, extent, cuts, -0.22, 0.18) * array
    return jnp.clip(array, min=-reach, max=reach).astype(held_as)


def setup_inputs(seed: int = 0) -> dict:
    splits = jax.random.split(jax.random.key(seed), 10)
    return {
        "vectors_in": bell_draw(splits[0], (M, NB), 1.0, 6.0, ((0, 16), (1, 2))),
        "panel": bell_draw(splits[1], (M, NPAN), M ** -0.5, 0.03125, ((0, 16), (1, 2))),
        "factor": draw_factor(jax.random.fold_in(splits[9], 71), 0),
        "atom_basis": jax.vmap(lambda own: ragged(own, A_DEV, M_DEV, BMAX, 0))(jax.random.split(splits[3], N_ROW)).reshape((N_ROW, A_DEV)).astype(jnp.int32),
        "proj_count": place_ends(jax.random.randint(splits[4], (ATOMS,), 1, NPMAX + 1), jax.random.fold_in(splits[4], 1), 1, NPMAX).astype(jnp.int32),
        "coupling": bell_draw(splits[5], (ATOMS, K, NPMAX * BMAX), (K * BMAX) ** -0.5, 0.4375, ((0, 16),)),
        "block_present": place_ends((jax.random.randint(splits[6], (ATOMS, K), 0, 4) < 3).astype(jnp.int32), jax.random.fold_in(splits[6], 1), 0, 1),
        "occ_mask": place_ends((jax.random.randint(splits[7], (NB,), 0, 4) < 3).astype(jnp.int32), jax.random.fold_in(splits[7], 1), 0, 1),
        "occ_weight": jnp.clip(jnp.exp(math.log(2.0) - 1.3862944 * jax.random.uniform(splits[8], (NB,), jnp.float32) ** steps_of(splits[8], (NB,), ((0, 2),), -0.2, 0.2)), 0.5, 2.0),
    }


def reference(vectors_in, panel, factor, atom_basis, proj_count, coupling, block_present, occ_mask, occ_weight):
    column_blocks = vectors_in.reshape(N_ROW, M_DEV, NB)
    panel_blocks = panel.reshape(N_ROW, M_DEV, NPAN)

    def accumulate(running, pair):
        product = lax.dot_general(pair[1], pair[0], (((0,), (0,)), ((), ())), preferred_element_type=jnp.float32)
        return running + product, None

    inner_products, leftover = lax.scan(accumulate, jnp.zeros((NPAN, NB), jnp.float32), (column_blocks, panel_blocks))
    mixing = jnp.dot(factor.T, inner_products, precision=lax.Precision.HIGHEST).astype(jnp.bfloat16)

    def rotate(pair):
        update = jnp.dot(pair[1], mixing, preferred_element_type=jnp.float32)
        return (pair[0].astype(jnp.float32) - update).astype(jnp.bfloat16)

    vectors = lax.map(rotate, (column_blocks, panel_blocks)).reshape(N_ROW * M_DEV, NB)

    counts = atom_basis.astype(jnp.int32)
    starts = jnp.cumsum(counts, axis=1).astype(jnp.int32) - counts
    starts = starts + jnp.arange(N_ROW, dtype=jnp.int32)[:, None] * M_DEV
    starts = starts.reshape(-1)
    counts_flat = counts.reshape(-1)
    slot_rank = jnp.arange(BMAX, dtype=jnp.int32)
    row_index = jnp.where(slot_rank[None, :] < counts_flat[:, None], starts[:, None] + slot_rank[None, :], N_ROW * M_DEV).astype(jnp.int32).reshape(-1)
    kept_rows = (jnp.arange(NPMAX, dtype=jnp.int32)[None, :] < proj_count[:, None]).astype(jnp.float32)
    weights = occ_mask.astype(jnp.float32) * occ_weight / NB
    rim_width = (K - 1) // 2

    def column_block(running, block_number):
        columns = lax.dynamic_slice_in_dim(vectors, block_number * NB_DEV, NB_DEV, 1)
        padded = jnp.take(columns, row_index, axis=0, mode="fill", fill_value=0).reshape(ATOMS, BMAX, NB_DEV).astype(jnp.float32)
        projections = jnp.zeros((ATOMS, NPMAX, NB_DEV), jnp.float32)
        for relative in range(K):
            blocks = coupling[:, relative].reshape(ATOMS, NPMAX, BMAX)
            blocks = jnp.where(block_present[:, relative, None, None] > 0, blocks, jnp.zeros_like(blocks)).astype(jnp.float32)
            neighbours = jnp.roll(padded, rim_width - relative, axis=0)
            projections = projections + jnp.einsum("aij,ajn->ain", blocks, neighbours, precision=lax.Precision.HIGHEST)
        rounded = (projections * kept_rows[:, :, None]).astype(jnp.bfloat16)
        local_weights = lax.dynamic_slice_in_dim(weights, block_number * NB_DEV, NB_DEV, 0)
        weighted = (rounded.astype(jnp.float32) * local_weights[None, None, :]).astype(jnp.bfloat16)
        partial_value = jnp.einsum("ain,ajn->aij", weighted.astype(jnp.float32), rounded.astype(jnp.float32), precision=lax.Precision.HIGHEST)
        return running + partial_value.reshape(ATOMS, NPMAX * NPMAX), None

    density, remains = lax.scan(column_block, jnp.zeros((ATOMS, NPMAX * NPMAX), jnp.float32), jnp.arange(N_COL, dtype=jnp.int32))
    return vectors, density
```

```python
import functools

import jax
import jax.numpy as jnp
import numpy as np
from jax import lax
from jax.experimental import pallas as pl
from jax.experimental.pallas import tpu as pltpu
from jax.sharding import PartitionSpec as P

NPMAX = 16
BMAX = 24
K = 9
RIM = (K - 1) // 2
HALO = RIM * BMAX
GROUP = 8
WIN = (GROUP + K - 1) * BMAX
F32 = jnp.float32
BF16 = jnp.bfloat16
MESH = pl.DeviceIdType.MESH


def mix_kernel(n, vec_hbm, panel_ref, factor_ref, cm_ref, spread_ref, fold_ref,
               mix_ref, pan_ref, halo_ref, band_ref,
               vec, part, got, load_sem, own_sem, pan_sems, halo_sems, inner_sems, mix_sems):
    row, col = lax.axis_index("row"), lax.axis_index("col")
    other = 1 - col
    up, down = lax.rem(row + 1, n), lax.rem(row + n - 1, n)
    rows = panel_ref.shape[0]
    half = panel_ref.shape[1]
    slab = mix_ref.shape[0] // n

    loads = pltpu.make_async_copy(vec_hbm, vec, load_sem)
    loads.start()
    own = pltpu.make_async_copy(panel_ref, pan_ref.at[col, pl.ds(HALO, rows)], own_sem)
    own.start()

    barrier = pltpu.get_barrier_semaphore()
    for step in range(1, n):
        peer = lax.rem(row + step, n)
        pl.semaphore_signal(barrier, inc=1, device_id=(peer, col), device_id_type=MESH)
    for peer in (row, up, down):
        pl.semaphore_signal(barrier, inc=1, device_id=(peer, other), device_id_type=MESH)
    pl.semaphore_wait(barrier, n - 1 + 3)

    def remote(src, dst, sems, slot, target):
        return pltpu.make_async_remote_copy(
            src_ref=src, dst_ref=dst, send_sem=sems.at[(0,) + slot], recv_sem=sems.at[(1,) + slot],
            device_id=target, device_id_type=MESH)

    swap = remote(panel_ref, pan_ref.at[col, pl.ds(HALO, rows)], pan_sems, (0,), (row, other))
    swap.start()
    halos = []
    for side, target in ((0, up), (1, down)):
        src_at = rows - HALO if side == 0 else 0
        dst_at = 0 if side == 0 else HALO + rows
        for where in (0, 1):
            to = col if where == 0 else other
            halos.append(remote(panel_ref.at[pl.ds(src_at, HALO)], pan_ref.at[col, pl.ds(dst_at, HALO)],
                                pan_sems, (1 + 2 * side + where,), (target, to)))
        halos.append(remote(vec_hbm.at[pl.ds(src_at, HALO)], halo_ref.at[side], halo_sems, (side,), (target, col)))
    loads.wait()

    def product(which, source):
        piece = lax.dot_general(source, vec[...], (((0,), (0,)), ((), ())), preferred_element_type=F32)
        part[which] = piece.T.astype(BF16)

    def inner_copy(which, step):
        peer = lax.rem(row + step, n)
        return remote(part.at[which, pl.ds(pl.multiple_of(peer * slab, slab), slab)],
                      got.at[which, step], inner_sems, (which, step), (peer, col))

    product(col, panel_ref[...])
    for step in range(1, n):
        inner_copy(col, step).start()
    swap.wait_recv()
    product(other, pan_ref[other, HALO:HALO + rows, :])
    for step in range(1, n):
        inner_copy(other, step).start()
    for copy in halos:
        copy.start()

    atoms = cm_ref.shape[1]

    def band_step(t, carry):
        acc = None
        lane = lax.broadcasted_iota(jnp.int32, (2 * GROUP * NPMAX, fold_ref.shape[1]), 1)
        for k in range(K):
            block = cm_ref[k, pl.ds(pl.multiple_of(t * 2 * GROUP, 2 * GROUP), 2 * GROUP), :].astype(F32)
            block = jnp.broadcast_to(block[:, None, :], (2 * GROUP, NPMAX, block.shape[1]))
            block = block.reshape(2 * GROUP * NPMAX, block.shape[2]) * spread_ref[...]
            folded = jnp.dot(block.astype(BF16), fold_ref[...], preferred_element_type=F32)
            inside = (lane >= k * BMAX) & (lane < (k + 1) * BMAX)
            acc = jnp.where(inside, folded, 0.0 if acc is None else acc)
        acc = jnp.concatenate([acc, jnp.zeros((acc.shape[0], WIN - acc.shape[1]), F32)], axis=1)
        for g in range(2):
            pieces = []
            for a in range(GROUP):
                at = (g * GROUP + a) * NPMAX
                piece = acc[at:at + NPMAX]
                pieces.append(piece if a == 0 else pltpu.roll(piece, a * BMAX, 1))
            band_ref[2 * t + g] = jnp.concatenate(pieces, axis=0).astype(BF16)
        return carry

    lax.fori_loop(0, atoms // (2 * GROUP), band_step, 0)

    mine = pl.ds(pl.multiple_of(row * slab, slab), slab)
    sums = []
    for which in (0, 1):
        sums.append(part[which, mine, :].astype(F32))
    for step in range(1, n):
        for which in (0, 1):
            inner_copy(which, step).wait_recv()
            sums[which] = sums[which] + got[which, step].astype(F32)
    inner = jnp.concatenate(sums, axis=1)
    mixed = jnp.dot(inner, factor_ref[...], precision=lax.Precision.HIGHEST, preferred_element_type=F32)
    mix_ref[mine, :] = mixed.astype(BF16)

    def mix_copy(step):
        peer = lax.rem(row + step, n)
        return remote(mix_ref.at[mine], mix_ref.at[mine], mix_sems, (step,), (peer, col))

    for step in range(1, n):
        mix_copy(step).start()
    own.wait()
    swap.wait_send()
    for copy in halos:
        copy.wait()
    for step in range(1, n):
        for which in (0, 1):
            inner_copy(which, step).wait_send()
    for step in range(1, n):
        mix_copy(step).wait()


def density_kernel(tiles, starts_ref, vin_ref, halo_ref, pan_ref, mix_ref, band_ref, weight_ref, expand_ref,
                   vec_ref, den_ref, ext, padded):
    step = pl.program_id(0)
    tile = vin_ref.shape[0]
    rows = tile * tiles

    def rotate(at, count, columns):
        panel = jnp.concatenate([pan_ref[0, pl.ds(at, count), :], pan_ref[1, pl.ds(at, count), :]], axis=1)
        update = lax.dot_general(panel, mix_ref[...], (((1,), (1,)), ((), ())), preferred_element_type=F32)
        return (columns.astype(F32) - update).astype(BF16)

    def keep(at, count, values):
        values = values.astype(F32)
        for c in range(ext.shape[0]):
            ext[c, pl.ds(at, count), :] = values[:, c * 128:(c + 1) * 128]

    @pl.when(step == 0)
    def _():
        keep(0, HALO, rotate(0, HALO, halo_ref[0]))
        keep(HALO + rows, HALO, rotate(HALO + rows, HALO, halo_ref[1]))
        spare = ext.shape[1] - 2 * HALO - rows
        ext[:, 2 * HALO + rows:, :] = jnp.zeros((ext.shape[0], spare, ext.shape[2]), F32)

    @pl.when(step < tiles)
    def _():
        at = pl.multiple_of(HALO + step * tile, 16)
        fresh = rotate(at, tile, vin_ref[...])
        vec_ref[...] = fresh
        keep(at, tile, fresh)

    @pl.when(step >= tiles)
    def _():
        j = step - tiles
        for pair in range(GROUP // 2):
            at = pl.multiple_of((j * GROUP + 2 * pair) * BMAX, 16)
            begins = [starts_ref[j * GROUP + 2 * pair + e] for e in (0, 1)]
            for c in range(ext.shape[0]):
                both = [ext[c, pl.ds(begin, BMAX), :] for begin in begins]
                both = jnp.concatenate(both, axis=0).astype(BF16)
                padded[pl.ds(at, 2 * BMAX), c * 128:(c + 1) * 128] = both

    @pl.when(step > tiles)
    def _():
        g = step - tiles - 1
        window = padded[pl.ds(pl.multiple_of(g * GROUP * BMAX, 16), WIN), :]
        rounded = jnp.dot(band_ref[0], window, preferred_element_type=F32).astype(BF16)
        weighted = (rounded.astype(F32) * weight_ref[...]).astype(BF16)
        full = lax.dot_general(weighted, rounded, (((1,), (1,)), ((), ())), preferred_element_type=F32)
        shape = full.shape
        own = lax.broadcasted_iota(jnp.int32, shape, 0) >> 4 == lax.broadcasted_iota(jnp.int32, shape, 1) >> 4
        full = jnp.where(own, full, 0.0)
        wide = jnp.dot(full, expand_ref[...], precision=lax.Precision.HIGHEST, preferred_element_type=F32)
        shape = wide.shape
        pick = (lax.broadcasted_iota(jnp.int32, shape, 0) & 15) == lax.broadcasted_iota(jnp.int32, shape, 1) >> 4
        wide = jnp.where(pick, wide, 0.0)
        den_ref[...] = wide.reshape(GROUP, NPMAX, wide.shape[1]).sum(axis=1)


def local(vectors_in, panel, factor, atom_basis, proj_count, coupling, block_present, occ_mask, occ_weight):
    n = lax.axis_size("row")
    rows, cols = vectors_in.shape
    half = panel.shape[1]
    npan = factor.shape[0]
    counts = atom_basis[0]
    atoms = counts.shape[0]
    groups = atoms // GROUP
    upward = [(i, (i + 1) % n) for i in range(n)]
    downward = [(j, i) for i, j in upward]
    before = lax.ppermute(counts[atoms - RIM:], "row", upward)
    after = lax.ppermute(counts[:RIM], "row", downward)
    counts_ext = jnp.concatenate([before, counts, after])
    starts = jnp.cumsum(counts_ext) - counts_ext + (HALO - jnp.sum(before))

    reach = jnp.stack([counts_ext[k:k + atoms] for k in range(K)], axis=0)
    reach = jnp.where(block_present.T > 0, reach, 0)
    lane = np.arange(NPMAX * BMAX)
    slot = jnp.asarray(lane % BMAX, jnp.int32)
    proj = jnp.asarray(lane // BMAX, jnp.int32)
    keep = (slot[None, None, :] < reach[:, :, None]) & (proj[None, None, :] < proj_count[None, :, None])
    cm = jnp.where(keep, jnp.swapaxes(coupling, 0, 1), jnp.zeros((), BF16))

    spread = jnp.asarray((lane[None, :] // BMAX) == (np.arange(2 * GROUP * NPMAX)[:, None] % NPMAX), F32)
    wide = np.arange(256)
    fold = jnp.asarray(((lane[:, None] % BMAX) == (wide[None, :] % BMAX)) & (wide[None, :] < K * BMAX), BF16)
    expand = jnp.asarray(
        (np.arange(GROUP * NPMAX)[:, None] % NPMAX) == (np.arange(NPMAX * NPMAX)[None, :] % NPMAX), F32)

    vmem = pl.BlockSpec(memory_space=pltpu.VMEM)
    slab = cols // n
    ext_rows = rows + 2 * HALO
    mix, pan, halo, band = pl.pallas_call(
        functools.partial(mix_kernel, n),
        out_shape=(
            jax.ShapeDtypeStruct((cols, npan), BF16),
            jax.ShapeDtypeStruct((2, ext_rows, half), BF16),
            jax.ShapeDtypeStruct((2, HALO, cols), BF16),
            jax.ShapeDtypeStruct((groups, GROUP * NPMAX, WIN), BF16),
        ),
        in_specs=[pl.BlockSpec(memory_space=pl.ANY)] + [vmem] * 5,
        out_specs=(vmem,) * 4,
        scratch_shapes=[
            pltpu.VMEM((rows, cols), BF16),
            pltpu.VMEM((2, cols, half), BF16),
            pltpu.VMEM((2, n, slab, half), BF16),
            pltpu.SemaphoreType.DMA,
            pltpu.SemaphoreType.DMA,
            pltpu.SemaphoreType.DMA((2, 5)),
            pltpu.SemaphoreType.DMA((2, 2)),
            pltpu.SemaphoreType.DMA((2, 2, n)),
            pltpu.SemaphoreType.DMA((2, n)),
        ],
        compiler_params=pltpu.CompilerParams(collective_id=0, has_side_effects=True, vmem_limit_bytes=40 << 20),
        cost_estimate=pl.CostEstimate(flops=8 * 10**9, bytes_accessed=10 << 20, transcendentals=0),
    )(vectors_in, panel, factor, cm, spread, fold)

    weights = occ_mask.astype(F32) * occ_weight / (cols * lax.axis_size("col"))
    tiles = 8
    tile = rows // tiles
    const = lambda *shape: pl.BlockSpec(shape, lambda s, st: (0,) * len(shape))
    vectors, partial = pl.pallas_call(
        functools.partial(density_kernel, tiles),
        out_shape=(
            jax.ShapeDtypeStruct((rows, cols), BF16),
            jax.ShapeDtypeStruct((atoms, NPMAX * NPMAX), F32),
        ),
        grid_spec=pltpu.PrefetchScalarGridSpec(
            num_scalar_prefetch=1,
            grid=(tiles + groups + 1,),
            in_specs=[
                pl.BlockSpec((tile, cols), lambda s, st: (jnp.minimum(s, tiles - 1), 0)),
                const(2, HALO, cols),
                const(2, ext_rows, half),
                const(cols, npan),
                pl.BlockSpec((1, GROUP * NPMAX, WIN), lambda s, st: (jnp.maximum(s - tiles - 1, 0), 0, 0)),
                const(1, cols),
                const(GROUP * NPMAX, NPMAX * NPMAX),
            ],
            out_specs=[
                pl.BlockSpec((tile, cols), lambda s, st: (jnp.minimum(s, tiles - 1), 0)),
                pl.BlockSpec((GROUP, NPMAX * NPMAX), lambda s, st: (jnp.maximum(s - tiles - 1, 0), 0)),
            ],
            scratch_shapes=[
                pltpu.VMEM((cols // 128, ext_rows + BMAX, 128), F32),
                pltpu.VMEM(((atoms + 2 * RIM) * BMAX, cols), BF16),
            ],
        ),
        compiler_params=pltpu.CompilerParams(vmem_limit_bytes=48 << 20),
        cost_estimate=pl.CostEstimate(flops=6 * 10**9, bytes_accessed=10 << 20, transcendentals=0),
    )(starts, vectors_in, halo, pan, mix, band, weights[None, :], expand)

    ncol = lax.axis_size("col")
    share = atoms // ncol
    col = lax.axis_index("col")
    density = lax.dynamic_slice_in_dim(partial, col * share, share, 0)
    for step in range(1, ncol):
        sent = lax.dynamic_slice_in_dim(partial, lax.rem(col + step, ncol) * share, share, 0)
        density = density + lax.ppermute(sent, "col", [(i, (i + step) % ncol) for i in range(ncol)])
    return (vectors, density)


def solution(mesh):
    placed = (
        P("row", "col"),
        P("row", "col"),
        P(),
        P("row", None),
        P("row"),
        P("row", None, None),
        P("row", None),
        P("col"),
        P("col"),
    )
    return jax.shard_map(
        local,
        mesh=mesh,
        in_specs=placed,
        out_specs=(P("row", "col"), P(("row", "col"), None)),
        check_vma=False,
    )
```

```python
import functools

import jax
import jax.numpy as jnp
from jax import lax
from jax.experimental import pallas as pl
from jax.experimental.pallas import tpu as pltpu
from jax.sharding import PartitionSpec as P

NPMAX = 16
BMAX = 24
K = 9
RIM = (K - 1) // 2
HALO = RIM * BMAX
GROUP = 16
WIN = -(-(GROUP + K - 1) * BMAX // 128) * 128
FOLD = -(-K * BMAX // 128) * 128
TILES = 4
F32 = jnp.float32
BF16 = jnp.bfloat16
MESH = pl.DeviceIdType.MESH


def iota(rows, columns, axis):
    return lax.broadcasted_iota(jnp.int32, (rows, columns), axis)


def group_of(rows, columns, axis, size, most):
    small = (8, columns) if axis == 1 else (rows, 128)
    index = iota(*small, axis)
    group = jnp.zeros(small, jnp.int32)
    for edge in range(1, most):
        group = group + jnp.where(index >= edge * size, 1, 0)
    return jnp.tile(group, (rows // small[0], columns // small[1]))


def mix_kernel(n, vec_hbm, panel_ref, factor_ref, basis_ref, proj_ref, cm_ref, present_ref,
               mix_ref, pan_ref, halo_ref, band_ref, start_ref,
               vec, part, got, counts, limit, spread, fold, load_sem, own_sem, pan_sems, halo_sems, count_sems, inner_sems, mix_sems):
    row, col = lax.axis_index("row"), lax.axis_index("col")
    other = 1 - col
    up, down = lax.rem(row + 1, n), lax.rem(row + n - 1, n)
    rows = panel_ref.shape[0]
    half = panel_ref.shape[1]
    slab = mix_ref.shape[0] // n

    loads = pltpu.make_async_copy(vec_hbm, vec, load_sem)
    loads.start()
    own = pltpu.make_async_copy(panel_ref, pan_ref.at[col, pl.ds(HALO, rows)], own_sem)
    own.start()

    barrier = pltpu.get_barrier_semaphore()
    for step in range(1, n):
        peer = lax.rem(row + step, n)
        pl.semaphore_signal(barrier, inc=1, device_id=(peer, col), device_id_type=MESH)
    for peer in (row, up, down):
        pl.semaphore_signal(barrier, inc=1, device_id=(peer, other), device_id_type=MESH)
    pl.semaphore_wait(barrier, n - 1 + 3)

    def remote(src, dst, sems, slot, target):
        return pltpu.make_async_remote_copy(
            src_ref=src, dst_ref=dst, send_sem=sems.at[(0,) + slot], recv_sem=sems.at[(1,) + slot],
            device_id=target, device_id_type=MESH)

    swap = remote(panel_ref, pan_ref.at[col, pl.ds(HALO, rows)], pan_sems, (0,), (row, other))
    swap.start()
    count_copies = [
        remote(basis_ref, counts.at[side], count_sems, (side,), (target, col))
        for side, target in ((0, up), (1, down))
    ]
    for copy in count_copies:
        copy.start()
    halos = []
    for side, target in ((0, up), (1, down)):
        src_at = rows - HALO if side == 0 else 0
        dst_at = 0 if side == 0 else HALO + rows
        for where in (0, 1):
            to = col if where == 0 else other
            halos.append(remote(panel_ref.at[pl.ds(src_at, HALO)], pan_ref.at[col, pl.ds(dst_at, HALO)],
                                pan_sems, (1 + 2 * side + where,), (target, to)))
        halos.append(remote(vec_hbm.at[pl.ds(src_at, HALO)], halo_ref.at[side], halo_sems, (side,), (target, col)))
    loads.wait()

    def product(which, source):
        piece = lax.dot_general(source, vec[...], (((0,), (0,)), ((), ())), preferred_element_type=F32)
        part[which] = piece.T.astype(BF16)

    def inner_copy(which, step):
        peer = lax.rem(row + step, n)
        return remote(part.at[which, pl.ds(pl.multiple_of(peer * slab, slab), slab)],
                      got.at[which, step], inner_sems, (which, step), (peer, col))

    product(col, panel_ref[...])
    for step in range(1, n):
        inner_copy(col, step).start()
    swap.wait_recv()
    product(other, pan_ref[other, HALO:HALO + rows, :])
    for step in range(1, n):
        inner_copy(other, step).start()
    for copy in halos:
        copy.start()

    atoms = cm_ref.shape[1]
    wide = cm_ref.shape[2]
    spread[...] = jnp.where(group_of(GROUP * NPMAX, wide, 1, BMAX, NPMAX) == (iota(GROUP * NPMAX, wide, 0) & 15),
                            1.0, 0.0)
    fold_slot = iota(wide, FOLD, 1) - BMAX * group_of(wide, FOLD, 1, BMAX, K)
    fold_from = iota(wide, FOLD, 0) - BMAX * group_of(wide, FOLD, 0, BMAX, NPMAX)
    fold[...] = jnp.where((fold_slot == fold_from) & (iota(wide, FOLD, 1) < K * BMAX), 1.0, 0.0).astype(BF16)
    for copy in count_copies:
        copy.wait_recv()
    here = basis_ref[...].astype(F32)
    prev, post = counts[0].astype(F32), counts[1].astype(F32)
    lower = jnp.where(iota(atoms, atoms, 0) < iota(atoms, atoms, 1), 1.0, 0.0).astype(BF16)
    table = jnp.concatenate([prev, here, post, jnp.zeros((5, atoms), F32)], axis=0).astype(BF16)
    first = jnp.dot(table, lower, preferred_element_type=F32).astype(jnp.int32)
    start_ref[...] = first + (HALO - rows) + rows * iota(8, atoms, 0)
    lines = []
    at = iota(1, atoms, 1)
    for k in range(K):
        d = k - RIM
        near = here
        if d != 0:
            turn = (-d) % atoms
            inside = (at + d >= 0) & (at + d < atoms)
            near = jnp.where(inside, pltpu.roll(here, turn, 1), pltpu.roll(prev if d < 0 else post, turn, 1))
        lines.append(jnp.where(present_ref[k:k + 1, :] > 0, near, 0.0))
    lines.append(proj_ref[...].astype(F32))
    lines.append(jnp.zeros((atoms - K - 1, atoms), F32))
    limit[...] = jnp.concatenate(lines, axis=0).T

    lane = iota(GROUP, FOLD, 1)
    in_k = group_of(GROUP, FOLD, 1, BMAX, K)
    slot = (lane - BMAX * in_k).astype(F32)

    def band_step(t, carry):
        chunk = pl.ds(pl.multiple_of(t * GROUP, GROUP), GROUP)
        bounds = limit[chunk, :]
        reach = jnp.zeros((GROUP, FOLD), F32)
        for k in range(K):
            reach = jnp.where(in_k == k, bounds[:, k:k + 1], reach)
        kept = jnp.where(slot < reach, 1.0, 0.0)
        kept = jnp.broadcast_to(kept[:, None, :], (GROUP, NPMAX, FOLD)).reshape(GROUP * NPMAX, FOLD)
        most = jnp.broadcast_to(bounds[:, K:K + 1], (GROUP, FOLD))
        most = jnp.broadcast_to(most[:, None, :], (GROUP, NPMAX, FOLD)).reshape(GROUP * NPMAX, FOLD)
        valid = (kept > 0.5) & ((iota(GROUP * NPMAX, FOLD, 0) & 15).astype(F32) < most)
        which_k = group_of(GROUP * NPMAX, FOLD, 1, BMAX, K)
        acc = jnp.zeros((GROUP * NPMAX, FOLD), F32)
        for k in range(K):
            block = cm_ref[k, chunk, :].astype(F32)
            block = jnp.broadcast_to(block[:, None, :], (GROUP, NPMAX, wide)).reshape(GROUP * NPMAX, wide)
            folded = jnp.dot((block * spread[...]).astype(BF16), fold[...], preferred_element_type=F32)
            acc = jnp.where(which_k == k, folded, acc)
        acc = jnp.where(valid, acc, 0.0)
        acc = jnp.concatenate([acc, jnp.zeros((acc.shape[0], WIN - FOLD), F32)], axis=1)
        pieces = []
        for a in range(GROUP):
            piece = acc[a * NPMAX:(a + 1) * NPMAX]
            pieces.append(piece if a == 0 else pltpu.roll(piece, a * BMAX, 1))
        band_ref[t] = jnp.concatenate(pieces, axis=0).astype(BF16)
        return carry

    lax.fori_loop(0, atoms // GROUP, band_step, 0)

    mine = pl.ds(pl.multiple_of(row * slab, slab), slab)
    sums = []
    for which in (0, 1):
        sums.append(part[which, mine, :].astype(F32))
    for step in range(1, n):
        for which in (0, 1):
            inner_copy(which, step).wait_recv()
            sums[which] = sums[which] + got[which, step].astype(F32)
    inner = jnp.concatenate(sums, axis=1)
    mixed = jnp.dot(inner, factor_ref[...], precision=lax.Precision.HIGHEST, preferred_element_type=F32)
    mix_ref[mine, :] = mixed.astype(BF16)

    def mix_copy(step):
        peer = lax.rem(row + step, n)
        return remote(mix_ref.at[mine], mix_ref.at[mine], mix_sems, (step,), (peer, col))

    for step in range(1, n):
        mix_copy(step).start()
    own.wait()
    swap.wait_send()
    for copy in count_copies:
        copy.wait_send()
    for copy in halos:
        copy.wait()
    for step in range(1, n):
        for which in (0, 1):
            inner_copy(which, step).wait_send()
    for step in range(1, n):
        mix_copy(step).wait()


def density_kernel(starts_ref, vin_ref, halo_ref, pan_ref, mix_ref, band_ref, mask_ref, occ_ref,
                   vec_ref, den_ref, ext, padded, mixing, weight, *, column_total):
    step = pl.program_id(0)
    tile = vin_ref.shape[0]
    rows = tile * TILES
    atoms = (padded.shape[0] - (WIN - (GROUP + K - 1) * BMAX)) // BMAX - 2 * RIM

    def rotate(at, count, columns):
        panel = jnp.concatenate([pan_ref[0, pl.ds(at, count), :], pan_ref[1, pl.ds(at, count), :]], axis=1)
        update = jnp.dot(panel, mixing[...], preferred_element_type=F32)
        return (columns.astype(F32) - update).astype(BF16)

    def keep(at, count, values):
        values = values.astype(F32)
        for c in range(ext.shape[0]):
            ext[c, pl.ds(at, count), :] = values[:, c * 128:(c + 1) * 128]

    def gather(atom, count):
        for pair in range(count // 2):
            at = pl.multiple_of((atom + 2 * pair) * BMAX, 16)
            begins = []
            for e in (0, 1):
                flat = atom + 2 * pair + e + atoms - RIM
                begins.append(starts_ref[lax.div(flat, atoms), lax.rem(flat, atoms)])
            for c in range(ext.shape[0]):
                both = [ext[c, pl.ds(begin, BMAX), :] for begin in begins]
                both = jnp.concatenate(both, axis=0).astype(BF16)
                padded[pl.ds(at, 2 * BMAX), c * 128:(c + 1) * 128] = both

    @pl.when(step == 0)
    def _():
        mixing[...] = mix_ref[...].T
        weight[...] = mask_ref[...].astype(F32) * occ_ref[...] / column_total
        keep(0, HALO, rotate(0, HALO, halo_ref[0]))
        keep(HALO + rows, HALO, rotate(HALO + rows, HALO, halo_ref[1]))
        spare = ext.shape[1] - 2 * HALO - rows
        ext[:, 2 * HALO + rows:, :] = jnp.zeros((ext.shape[0], spare, ext.shape[2]), F32)
        used = (atoms + 2 * RIM) * BMAX
        padded[used:, :] = jnp.zeros((padded.shape[0] - used, padded.shape[1]), BF16)

    @pl.when(step < TILES)
    def _():
        at = pl.multiple_of(HALO + step * tile, 16)
        fresh = rotate(at, tile, vin_ref[...])
        vec_ref[...] = fresh
        keep(at, tile, fresh)

    @pl.when(step == TILES - 1)
    def _():
        gather(0, 2 * RIM)

    @pl.when(step >= TILES)
    def _():
        g = step - TILES
        gather(g * GROUP + 2 * RIM, GROUP)
        window = padded[pl.ds(pl.multiple_of(g * GROUP * BMAX, 16), WIN), :]
        rounded = jnp.dot(band_ref[0], window, preferred_element_type=F32).astype(BF16)
        weighted = (rounded.astype(F32) * weight[...]).astype(BF16)
        full = lax.dot_general(weighted, rounded, (((1,), (1,)), ((), ())), preferred_element_type=F32)
        shape = full.shape
        full = jnp.where(iota(*shape, 0) >> 4 == iota(*shape, 1) >> 4, full, 0.0)
        expand = jnp.where((iota(shape[1], NPMAX * NPMAX, 0) & 15) == (iota(shape[1], NPMAX * NPMAX, 1) & 15),
                           1.0, 0.0).astype(BF16)
        spreads = 0.0
        for _ in range(3):
            top = full.astype(BF16)
            spreads = spreads + jnp.dot(top, expand, preferred_element_type=F32)
            full = full - top.astype(F32)
        shape = spreads.shape
        spreads = jnp.where((iota(*shape, 0) & 15) == iota(*shape, 1) >> 4, spreads, 0.0)
        den_ref[...] = spreads.reshape(GROUP, NPMAX, shape[1]).sum(axis=1)


def local(vectors_in, panel, factor, atom_basis, proj_count, coupling, block_present, occ_mask, occ_weight):
    n = lax.axis_size("row")
    rows, cols = vectors_in.shape
    half = panel.shape[1]
    npan = factor.shape[0]
    atoms = atom_basis.shape[1]
    groups = atoms // GROUP
    vmem = pl.BlockSpec(memory_space=pltpu.VMEM)
    slab = cols // n
    ext_rows = rows + 2 * HALO
    mix, pan, halo, band, starts = pl.pallas_call(
        functools.partial(mix_kernel, n),
        out_shape=(
            jax.ShapeDtypeStruct((cols, npan), BF16),
            jax.ShapeDtypeStruct((2, ext_rows, half), BF16),
            jax.ShapeDtypeStruct((2, HALO, cols), BF16),
            jax.ShapeDtypeStruct((groups, GROUP * NPMAX, WIN), BF16),
            jax.ShapeDtypeStruct((8, atoms), jnp.int32),
        ),
        in_specs=[pl.BlockSpec(memory_space=pltpu.HBM)] + [vmem] * 6,
        out_specs=(vmem,) * 5,
        scratch_shapes=[
            pltpu.VMEM((rows, cols), BF16),
            pltpu.VMEM((2, cols, half), BF16),
            pltpu.VMEM((2, n, slab, half), BF16),
            pltpu.VMEM((2, 1, atoms), jnp.int32),
            pltpu.VMEM((atoms, atoms), F32),
            pltpu.VMEM((GROUP * NPMAX, NPMAX * BMAX), F32),
            pltpu.VMEM((NPMAX * BMAX, FOLD), BF16),
            pltpu.SemaphoreType.DMA,
            pltpu.SemaphoreType.DMA,
            pltpu.SemaphoreType.DMA((2, 5)),
            pltpu.SemaphoreType.DMA((2, 2)),
            pltpu.SemaphoreType.DMA((2, 2)),
            pltpu.SemaphoreType.DMA((2, 2, n)),
            pltpu.SemaphoreType.DMA((2, n)),
        ],
        compiler_params=pltpu.CompilerParams(collective_id=0, has_side_effects=True, vmem_limit_bytes=40 << 20),
        cost_estimate=pl.CostEstimate(flops=8 * 10**9, bytes_accessed=10 << 20, transcendentals=0),
    )(vectors_in, panel, factor, atom_basis, proj_count[None, :], jnp.swapaxes(coupling, 0, 1), block_present.T)

    tile = rows // TILES
    const = lambda *shape: pl.BlockSpec(shape, lambda s, st: (0,) * len(shape))
    vectors, partial = pl.pallas_call(
        functools.partial(density_kernel, column_total=cols * lax.axis_size("col")),
        out_shape=(
            jax.ShapeDtypeStruct((rows, cols), BF16),
            jax.ShapeDtypeStruct((atoms, NPMAX * NPMAX), F32),
        ),
        grid_spec=pltpu.PrefetchScalarGridSpec(
            num_scalar_prefetch=1,
            grid=(TILES + groups,),
            in_specs=[
                pl.BlockSpec((tile, cols), lambda s, st: (jnp.minimum(s, TILES - 1), 0)),
                const(2, HALO, cols),
                const(2, ext_rows, half),
                const(cols, npan),
                pl.BlockSpec((1, GROUP * NPMAX, WIN), lambda s, st: (jnp.maximum(s - TILES, 0), 0, 0)),
                const(1, cols),
                const(1, cols),
            ],
            out_specs=[
                pl.BlockSpec((tile, cols), lambda s, st: (jnp.minimum(s, TILES - 1), 0)),
                pl.BlockSpec((GROUP, NPMAX * NPMAX), lambda s, st: (jnp.maximum(s - TILES, 0), 0)),
            ],
            scratch_shapes=[
                pltpu.VMEM((cols // 128, ext_rows + BMAX, 128), F32),
                pltpu.VMEM(((atoms + 2 * RIM) * BMAX + WIN - (GROUP + K - 1) * BMAX, cols), BF16),
                pltpu.VMEM((npan, cols), BF16),
                pltpu.VMEM((1, cols), F32),
            ],
        ),
        compiler_params=pltpu.CompilerParams(vmem_limit_bytes=48 << 20),
        cost_estimate=pl.CostEstimate(flops=6 * 10**9, bytes_accessed=10 << 20, transcendentals=0),
    )(starts, vectors_in, halo, pan, mix, band, occ_mask[None, :], occ_weight[None, :])

    ncol = lax.axis_size("col")
    share = atoms // ncol
    col = lax.axis_index("col")
    density = lax.dynamic_slice_in_dim(partial, col * share, share, 0)
    for step in range(1, ncol):
        sent = lax.dynamic_slice_in_dim(partial, lax.rem(col + step, ncol) * share, share, 0)
        density = density + lax.ppermute(sent, "col", [(i, (i + step) % ncol) for i in range(ncol)])
    return (vectors, density)


def solution(mesh):
    placed = (
        P("row", "col"),
        P("row", "col"),
        P(),
        P("row", None),
        P("row"),
        P("row", None, None),
        P("row", None),
        P("col"),
        P("col"),
    )
    return jax.shard_map(
        local,
        mesh=mesh,
        in_specs=placed,
        out_specs=(P("row", "col"), P(("row", "col"), None)),
        check_vma=False,
    )
```

```python
import functools

import jax
import jax.numpy as jnp
from jax import lax
from jax.experimental import pallas as pl
from jax.experimental.pallas import tpu as pltpu
from jax.sharding import PartitionSpec as P

NPMAX = 16
BMAX = 24
K = 9
RIM = (K - 1) // 2
HALO = RIM * BMAX
GROUP = 16
WIN = -(-(GROUP + K - 1) * BMAX // 128) * 128
FOLD = -(-K * BMAX // 128) * 128
F32 = jnp.float32
BF16 = jnp.bfloat16
MESH = pl.DeviceIdType.MESH


def iota(rows, columns, axis):
    return lax.broadcasted_iota(jnp.int32, (rows, columns), axis)


def group_of(rows, columns, axis, size, most):
    small = (8, columns) if axis == 1 else (rows, 128)
    index = iota(*small, axis)
    group = jnp.zeros(small, jnp.int32)
    for edge in range(1, most):
        group = group + jnp.where(index >= edge * size, 1, 0)
    return jnp.tile(group, (rows // small[0], columns // small[1]))


def mix_kernel(n, vec_hbm, panel_hbm, coupling_hbm, factor_ref, basis_ref, proj_ref, present_ref,
               mix_ref, pan_ref, base_ref, lean_ref,
               vec, part, got, counts, limit, spread, fold, cm_ref, halo_ref, band, first_ref, starts,
               ext, pext, padded, ppadded,
               load_sem, own_sem, cm_sem, start_sem, pan_sems, halo_sems, count_sems, inner_sems, mix_sems):
    row, col = lax.axis_index("row"), lax.axis_index("col")
    other = 1 - col
    up, down = lax.rem(row + 1, n), lax.rem(row + n - 1, n)
    rows, half = panel_hbm.shape
    slab = mix_ref.shape[0] // n
    body = pl.ds(HALO, rows)

    own = pltpu.make_async_copy(panel_hbm, pan_ref.at[col, body], own_sem)
    own.start()
    loads = pltpu.make_async_copy(vec_hbm, vec, load_sem)
    loads.start()
    blocks = pltpu.make_async_copy(coupling_hbm, cm_ref, cm_sem)
    blocks.start()

    barrier = pltpu.get_barrier_semaphore()
    for step in range(1, n):
        peer = lax.rem(row + step, n)
        pl.semaphore_signal(barrier, inc=1, device_id=(peer, col), device_id_type=MESH)
    for peer in (row, up, down):
        pl.semaphore_signal(barrier, inc=1, device_id=(peer, other), device_id_type=MESH)
    pl.semaphore_wait(barrier, n - 1 + 3)

    def remote(src, dst, sems, slot, target):
        return pltpu.make_async_remote_copy(
            src_ref=src, dst_ref=dst, send_sem=sems.at[(0,) + slot], recv_sem=sems.at[(1,) + slot],
            device_id=target, device_id_type=MESH)

    swap = remote(panel_hbm, pan_ref.at[col, pl.ds(HALO, rows)], pan_sems, (0,), (row, other))
    swap.start()
    count_copies = [
        remote(basis_ref, counts.at[side], count_sems, (side,), (target, col))
        for side, target in ((0, up), (1, down))
    ]
    for copy in count_copies:
        copy.start()
    halos = []
    for side, target in ((0, up), (1, down)):
        src_at = rows - HALO if side == 0 else 0
        dst_at = 0 if side == 0 else HALO + rows
        for where in (0, 1):
            to = col if where == 0 else other
            halos.append(remote(panel_hbm.at[pl.ds(src_at, HALO)], pan_ref.at[col, pl.ds(dst_at, HALO)],
                                pan_sems, (1 + 2 * side + where,), (target, to)))
        halos.append(remote(vec_hbm.at[pl.ds(src_at, HALO)], halo_ref.at[side], halo_sems, (side,), (target, col)))
    own.wait()
    loads.wait()

    def product(which, source):
        piece = lax.dot_general(source, vec[...], (((0,), (0,)), ((), ())), preferred_element_type=F32)
        part[which] = piece.T.astype(BF16)

    def inner_copy(which, step):
        peer = lax.rem(row + step, n)
        return remote(part.at[which, pl.ds(pl.multiple_of(peer * slab, slab), slab)],
                      got.at[which, step], inner_sems, (which, step), (peer, col))

    product(col, pan_ref[col, HALO:HALO + rows, :])
    for step in range(1, n):
        inner_copy(col, step).start()
    swap.wait_recv()
    product(other, pan_ref[other, HALO:HALO + rows, :])
    for step in range(1, n):
        inner_copy(other, step).start()
    for copy in halos:
        copy.start()

    atoms = cm_ref.shape[1]
    wide = cm_ref.shape[2]
    spread[...] = jnp.where(group_of(GROUP * NPMAX, wide, 1, BMAX, NPMAX) == (iota(GROUP * NPMAX, wide, 0) & 15),
                            1.0, 0.0)
    fold_slot = iota(wide, FOLD, 1) - BMAX * group_of(wide, FOLD, 1, BMAX, K)
    fold_from = iota(wide, FOLD, 0) - BMAX * group_of(wide, FOLD, 0, BMAX, NPMAX)
    fold[...] = jnp.where((fold_slot == fold_from) & (iota(wide, FOLD, 1) < K * BMAX), 1.0, 0.0).astype(BF16)
    for copy in count_copies:
        copy.wait_recv()
    blocks.wait()
    here = basis_ref[...].astype(F32)
    prev, post = counts[0].astype(F32), counts[1].astype(F32)
    lower = jnp.where(iota(atoms, atoms, 0) < iota(atoms, atoms, 1), 1.0, 0.0).astype(BF16)
    table = jnp.concatenate([prev, here, post, jnp.zeros((5, atoms), F32)], axis=0).astype(BF16)
    first = jnp.dot(table, lower, preferred_element_type=F32).astype(jnp.int32)
    first_ref[...] = jnp.clip(first + (HALO - rows) + rows * iota(8, atoms, 0), 0, rows + 2 * HALO)
    begin_copy = pltpu.make_async_copy(first_ref, starts, start_sem)
    begin_copy.start()
    lines = []
    at = iota(1, atoms, 1)
    for k in range(K):
        d = k - RIM
        near = here
        if d != 0:
            turn = (-d) % atoms
            inside = (at + d >= 0) & (at + d < atoms)
            near = jnp.where(inside, pltpu.roll(here, turn, 1), pltpu.roll(prev if d < 0 else post, turn, 1))
        lines.append(jnp.where(present_ref[k:k + 1, :] > 0, near, 0.0))
    lines.append(proj_ref[...].astype(F32))
    lines.append(jnp.zeros((atoms - K - 1, atoms), F32))
    limit[...] = jnp.concatenate(lines, axis=0).T

    lane = iota(GROUP, FOLD, 1)
    in_k = group_of(GROUP, FOLD, 1, BMAX, K)
    slot = (lane - BMAX * in_k).astype(F32)

    def band_step(t, carry):
        chunk = pl.ds(pl.multiple_of(t * GROUP, GROUP), GROUP)
        bounds = limit[chunk, :]
        reach = jnp.zeros((GROUP, FOLD), F32)
        for k in range(K):
            reach = jnp.where(in_k == k, bounds[:, k:k + 1], reach)
        kept = jnp.where(slot < reach, 1.0, 0.0)
        kept = jnp.broadcast_to(kept[:, None, :], (GROUP, NPMAX, FOLD)).reshape(GROUP * NPMAX, FOLD)
        most = jnp.broadcast_to(bounds[:, K:K + 1], (GROUP, FOLD))
        most = jnp.broadcast_to(most[:, None, :], (GROUP, NPMAX, FOLD)).reshape(GROUP * NPMAX, FOLD)
        valid = (kept > 0.5) & ((iota(GROUP * NPMAX, FOLD, 0) & 15).astype(F32) < most)
        which_k = group_of(GROUP * NPMAX, FOLD, 1, BMAX, K)
        acc = jnp.zeros((GROUP * NPMAX, FOLD), F32)
        for k in range(K):
            block = cm_ref[k, chunk, :].astype(F32)
            block = jnp.broadcast_to(block[:, None, :], (GROUP, NPMAX, wide)).reshape(GROUP * NPMAX, wide)
            folded = jnp.dot((block * spread[...]).astype(BF16), fold[...], preferred_element_type=F32)
            acc = jnp.where(which_k == k, folded, acc)
        acc = jnp.where(valid, acc, 0.0)
        acc = jnp.concatenate([acc, jnp.zeros((acc.shape[0], WIN - FOLD), F32)], axis=1)
        pieces = []
        for a in range(GROUP):
            piece = acc[a * NPMAX:(a + 1) * NPMAX]
            pieces.append(piece if a == 0 else pltpu.roll(piece, a * BMAX, 1))
        band[t] = jnp.concatenate(pieces, axis=0).astype(BF16)
        return carry

    lax.fori_loop(0, atoms // GROUP, band_step, 0)

    begin_copy.wait()
    for copy in halos:
        copy.wait()
    length = ext.shape[1]
    lanes = [slice(c * 128, (c + 1) * 128) for c in range(ext.shape[0])]
    chunk_rows = rows // 8

    def widen(t, carry):
        at = pl.multiple_of(t * chunk_rows, 16)
        block = vec[pl.ds(at, chunk_rows), :].astype(F32)
        for c, span in enumerate(lanes):
            ext[c, pl.ds(HALO + at, chunk_rows), :] = block[:, span]
        return carry

    lax.fori_loop(0, 8, widen, 0)
    for side, at in ((0, 0), (1, HALO + rows)):
        block = halo_ref[side].astype(F32)
        for c, span in enumerate(lanes):
            ext[c, at:at + HALO, :] = block[:, span]
    spare = length - 2 * HALO - rows
    ext[:, length - spare:, :] = jnp.zeros((ext.shape[0], spare, 128), F32)
    for which in (0, 1):
        pext[which, 0:length - spare, :] = pan_ref[which].astype(F32)
    pext[:, length - spare:, :] = jnp.zeros((2, spare, half), F32)
    used = (atoms + 2 * RIM) * BMAX
    padded[used:, :] = jnp.zeros((padded.shape[0] - used, padded.shape[1]), BF16)
    ppadded[used:, :] = jnp.zeros((ppadded.shape[0] - used, ppadded.shape[1]), BF16)

    def gather(t, carry):
        at = pl.multiple_of(2 * t * BMAX, 16)
        begins = []
        for e in (0, 1):
            flat = 2 * t + e + atoms - RIM
            begins.append(starts[lax.div(flat, atoms), lax.rem(flat, atoms)])
        for c, span in enumerate(lanes):
            both = [ext[c, pl.ds(begin, BMAX), :] for begin in begins]
            padded[pl.ds(at, 2 * BMAX), span] = jnp.concatenate(both, axis=0).astype(BF16)
        for c in (0, 1):
            both = [pext[c, pl.ds(begin, BMAX), :] for begin in begins]
            ppadded[pl.ds(at, 2 * BMAX), c * half:(c + 1) * half] = jnp.concatenate(both, axis=0).astype(BF16)
        return carry

    lax.fori_loop(0, (atoms + 2 * RIM) // 2, gather, 0)

    mine = pl.ds(pl.multiple_of(row * slab, slab), slab)
    sums = []
    for which in (0, 1):
        sums.append(part[which, mine, :].astype(F32))
    for step in range(1, n):
        for which in (0, 1):
            inner_copy(which, step).wait_recv()
            sums[which] = sums[which] + got[which, step].astype(F32)
    inner = jnp.concatenate(sums, axis=1)
    mixed = jnp.dot(inner, factor_ref[...], precision=lax.Precision.HIGHEST, preferred_element_type=F32)
    mix_ref[mine, :] = mixed.astype(BF16)

    def mix_copy(step):
        peer = lax.rem(row + step, n)
        return remote(mix_ref.at[mine], mix_ref.at[mine], mix_sems, (step,), (peer, col))

    for step in range(1, n):
        mix_copy(step).start()

    def project(g, carry):
        at = pl.ds(pl.multiple_of(g * GROUP * BMAX, 16), WIN)
        base_ref[g] = jnp.dot(band[g], padded[at, :], preferred_element_type=F32)
        lean_ref[g] = jnp.dot(band[g], ppadded[at, :], preferred_element_type=F32).astype(BF16)
        return carry

    lax.fori_loop(0, atoms // GROUP, project, 0)
    swap.wait_send()
    for copy in count_copies:
        copy.wait_send()
    for step in range(1, n):
        for which in (0, 1):
            inner_copy(which, step).wait_send()
    for step in range(1, n):
        mix_copy(step).wait()


def density_kernel(vin_ref, pan_ref, mix_ref, base_ref, lean_ref, mask_ref, occ_ref,
                   vec_ref, den_ref, mixing, weight, *, column_total):
    step = pl.program_id(0)
    tile = vin_ref.shape[0]

    @pl.when(step == 0)
    def _():
        mixing[...] = mix_ref[...].T
        weight[...] = mask_ref[...].astype(F32) * occ_ref[...] / column_total

    at = pl.ds(pl.multiple_of(HALO + step * tile, 16), tile)
    panel = jnp.concatenate([pan_ref[0, at, :], pan_ref[1, at, :]], axis=1)
    update = jnp.dot(panel, mixing[...], preferred_element_type=F32)
    vec_ref[...] = (vin_ref[...].astype(F32) - update).astype(BF16)
    update = jnp.dot(lean_ref[step], mixing[...], preferred_element_type=F32)
    rounded = (base_ref[step] - update).astype(BF16)
    weighted = (rounded.astype(F32) * weight[...]).astype(BF16)
    full = lax.dot_general(weighted, rounded, (((1,), (1,)), ((), ())), preferred_element_type=F32)
    shape = full.shape
    full = jnp.where(iota(*shape, 0) >> 4 == iota(*shape, 1) >> 4, full, 0.0)
    expand = jnp.where((iota(shape[1], NPMAX * NPMAX, 0) & 15) == (iota(shape[1], NPMAX * NPMAX, 1) & 15),
                       1.0, 0.0).astype(BF16)
    spreads = 0.0
    for _ in range(3):
        top = full.astype(BF16)
        spreads = spreads + jnp.dot(top, expand, preferred_element_type=F32)
        full = full - top.astype(F32)
    shape = spreads.shape
    spreads = jnp.where((iota(*shape, 0) & 15) == iota(*shape, 1) >> 4, spreads, 0.0)
    den_ref[...] = spreads.reshape(GROUP, NPMAX, shape[1]).sum(axis=1)


def local(vectors_in, panel, factor, atom_basis, proj_count, coupling, block_present, occ_mask, occ_weight):
    n = lax.axis_size("row")
    rows, cols = vectors_in.shape
    half = panel.shape[1]
    npan = factor.shape[0]
    atoms = atom_basis.shape[1]
    groups = atoms // GROUP
    vmem = pl.BlockSpec(memory_space=pltpu.VMEM)
    hbm = pl.BlockSpec(memory_space=pl.ANY)
    slab = cols // n
    ext_rows = rows + 2 * HALO
    pad_rows = (groups - 1) * GROUP * BMAX + WIN
    dma = pltpu.SemaphoreType.DMA
    operands = (vectors_in, panel, jnp.swapaxes(coupling, 0, 1), factor, atom_basis, proj_count[None, :], block_present.T)
    operands = [pltpu.with_memory_space_constraint(x, pltpu.HBM) for x in operands]
    mix, pan, base, lean = pl.pallas_call(
        functools.partial(mix_kernel, n),
        out_shape=(
            jax.ShapeDtypeStruct((cols, npan), BF16),
            jax.ShapeDtypeStruct((2, ext_rows, half), BF16),
            jax.ShapeDtypeStruct((groups, GROUP * NPMAX, cols), F32),
            jax.ShapeDtypeStruct((groups, GROUP * NPMAX, npan), BF16),
        ),
        in_specs=[hbm] * 3 + [vmem] * 4,
        out_specs=(vmem,) * 4,
        scratch_shapes=[
            pltpu.VMEM((rows, cols), BF16),
            pltpu.VMEM((2, cols, half), BF16),
            pltpu.VMEM((2, n, slab, half), BF16),
            pltpu.VMEM((2, 1, atoms), jnp.int32),
            pltpu.VMEM((atoms, atoms), F32),
            pltpu.VMEM((GROUP * NPMAX, NPMAX * BMAX), F32),
            pltpu.VMEM((NPMAX * BMAX, FOLD), BF16),
            pltpu.VMEM((K, atoms, NPMAX * BMAX), BF16),
            pltpu.VMEM((2, HALO, cols), BF16),
            pltpu.VMEM((groups, GROUP * NPMAX, WIN), BF16),
            pltpu.VMEM((8, atoms), jnp.int32),
            pltpu.SMEM((8, atoms), jnp.int32),
            pltpu.VMEM((cols // 128, ext_rows + BMAX, 128), F32),
            pltpu.VMEM((2, ext_rows + BMAX, half), F32),
            pltpu.VMEM((pad_rows, cols), BF16),
            pltpu.VMEM((pad_rows, npan), BF16),
            dma, dma, dma, dma, dma((2, 5)), dma((2, 2)), dma((2, 2)), dma((2, 2, n)), dma((2, n)),
        ],
        compiler_params=pltpu.CompilerParams(collective_id=0, has_side_effects=True, vmem_limit_bytes=40 << 20),
        cost_estimate=pl.CostEstimate(flops=8 * 10**9, bytes_accessed=10 << 20, transcendentals=0),
    )(*operands)

    tile = rows // groups
    vectors, partial = pl.pallas_call(
        functools.partial(density_kernel, column_total=cols * lax.axis_size("col")),
        out_shape=(
            jax.ShapeDtypeStruct((rows, cols), BF16),
            jax.ShapeDtypeStruct((atoms, NPMAX * NPMAX), F32),
        ),
        grid=(groups,),
        in_specs=[pl.BlockSpec((tile, cols), lambda s: (s, 0))] + [vmem] * 6,
        out_specs=[
            pl.BlockSpec((tile, cols), lambda s: (s, 0)),
            pl.BlockSpec((GROUP, NPMAX * NPMAX), lambda s: (s, 0)),
        ],
        scratch_shapes=[pltpu.VMEM((npan, cols), BF16), pltpu.VMEM((1, cols), F32)],
        compiler_params=pltpu.CompilerParams(vmem_limit_bytes=16 << 20),
        cost_estimate=pl.CostEstimate(flops=6 * 10**9, bytes_accessed=10 << 20, transcendentals=0),
    )(operands[0], pan, mix, base, lean, occ_mask[None, :], occ_weight[None, :])

    ncol = lax.axis_size("col")
    share = atoms // ncol
    col = lax.axis_index("col")
    density = lax.dynamic_slice_in_dim(partial, col * share, share, 0)
    for step in range(1, ncol):
        sent = lax.dynamic_slice_in_dim(partial, lax.rem(col + step, ncol) * share, share, 0)
        density = density + lax.ppermute(sent, "col", [(i, (i + step) % ncol) for i in range(ncol)])
    return (vectors, density)


def solution(mesh):
    placed = (
        P("row", "col"),
        P("row", "col"),
        P(),
        P("row", None),
        P("row"),
        P("row", None, None),
        P("row", None),
        P("col"),
        P("col"),
    )
    return jax.shard_map(
        local,
        mesh=mesh,
        in_specs=placed,
        out_specs=(P("row", "col"), P(("row", "col"), None)),
        check_vma=False,
    )
```

```python
import functools

import jax
import jax.numpy as jnp
from jax import lax
from jax.experimental import pallas as pl
from jax.experimental.pallas import tpu as pltpu
from jax.sharding import PartitionSpec as P

NPMAX = 16
BMAX = 24
K = 9
RIM = (K - 1) // 2
HALO = RIM * BMAX
GROUP = 16
WIN = -(-(GROUP + K - 1) * BMAX // 128) * 128
FOLD = -(-K * BMAX // 128) * 128
F32 = jnp.float32
BF16 = jnp.bfloat16
MESH = pl.DeviceIdType.MESH


def iota(rows, columns, axis):
    return lax.broadcasted_iota(jnp.int32, (rows, columns), axis)


def group_of(rows, columns, axis, size, most):
    small = (8, columns) if axis == 1 else (rows, 128)
    index = iota(*small, axis)
    group = jnp.zeros(small, jnp.int32)
    for edge in range(1, most):
        group = group + jnp.where(index >= edge * size, 1, 0)
    return jnp.tile(group, (rows // small[0], columns // small[1]))


def mix_kernel(n, plane, vec_hbm, panel_hbm, coupling_hbm, factor_ref, basis_ref, proj_ref, present_ref,
               mix_ref, pan_ref, base_ref, lean_ref,
               vec, part, got, middle, got_line, counts, limit, spread, fold, cm_ref, halo_ref, band, first_ref, starts,
               ext, pext, padded, ppadded,
               load_sem, own_sem, cm_sem, start_sem, pan_sems, halo_sems, count_sems, plane_sems, line_sems, mix_sems, pass_sems):
    row, col = lax.axis_index("row"), lax.axis_index("col")
    other = 1 - col
    up, down = lax.rem(row + 1, n), lax.rem(row + n - 1, n)
    rows, half = panel_hbm.shape
    slab = mix_ref.shape[0] // n
    body = pl.ds(HALO, rows)
    q, p = n // plane, plane
    line, spot = lax.div(row, p), lax.rem(row, p)

    def plane_peer(step):
        return line * p + lax.rem(spot + step, p)

    def line_peer(step):
        return lax.rem(line + step, q) * p + spot


    own = pltpu.make_async_copy(panel_hbm, pan_ref.at[col, body], own_sem)
    own.start()
    loads = pltpu.make_async_copy(vec_hbm, vec, load_sem)
    loads.start()
    blocks = pltpu.make_async_copy(coupling_hbm, cm_ref, cm_sem)
    blocks.start()

    barrier = pltpu.get_barrier_semaphore()
    greeted = [(plane_peer(step), col) for step in range(1, p)] + [(line_peer(step), col) for step in range(1, q)]
    greeted += [(up, col), (down, col)] + [(peer, other) for peer in (row, up, down)]
    for target in greeted:
        pl.semaphore_signal(barrier, inc=1, device_id=target, device_id_type=MESH)
    pl.semaphore_wait(barrier, len(greeted))

    def remote(src, dst, sems, slot, target):
        return pltpu.make_async_remote_copy(
            src_ref=src, dst_ref=dst, send_sem=sems.at[(0,) + slot], recv_sem=sems.at[(1,) + slot],
            device_id=target, device_id_type=MESH)

    swap = remote(panel_hbm, pan_ref.at[col, pl.ds(HALO, rows)], pan_sems, (0,), (row, other))
    swap.start()
    count_copies = [
        remote(basis_ref, counts.at[side], count_sems, (side,), (target, col))
        for side, target in ((0, up), (1, down))
    ]
    for copy in count_copies:
        copy.start()
    halos = []
    for side, target in ((0, up), (1, down)):
        src_at = rows - HALO if side == 0 else 0
        dst_at = 0 if side == 0 else HALO + rows
        for where in (0, 1):
            to = col if where == 0 else other
            halos.append(remote(panel_hbm.at[pl.ds(src_at, HALO)], pan_ref.at[col, pl.ds(dst_at, HALO)],
                                pan_sems, (1 + 2 * side + where,), (target, to)))
        halos.append(remote(vec_hbm.at[pl.ds(src_at, HALO)], halo_ref.at[side], halo_sems, (side,), (target, col)))
    own.wait()
    loads.wait()

    def product(which, source):
        piece = lax.dot_general(source, vec[...], (((0,), (0,)), ((), ())), preferred_element_type=F32)
        piece = piece.T.astype(BF16)
        for z in range(q):
            for at in range(p):
                part[which, at, z * slab:(z + 1) * slab] = piece[(z * p + at) * slab:(z * p + at + 1) * slab]

    def plane_copy(which, step):
        return remote(part.at[which, lax.rem(spot + step, p)], got.at[which, step], plane_sems, (which, step),
                      (plane_peer(step), col))

    def line_copy(which, step):
        at = pl.multiple_of(lax.rem(line + step, q) * slab, slab)
        return remote(middle.at[which, pl.ds(at, slab)], got_line.at[which, step], line_sems, (which, step),
                      (line_peer(step), col))

    product(col, pan_ref[col, HALO:HALO + rows, :])
    for step in range(1, p):
        plane_copy(col, step).start()
    swap.wait_recv()
    product(other, pan_ref[other, HALO:HALO + rows, :])
    for step in range(1, p):
        plane_copy(other, step).start()
    for copy in halos:
        copy.start()

    atoms = cm_ref.shape[1]
    wide = cm_ref.shape[2]
    spread[...] = jnp.where(group_of(GROUP * NPMAX, wide, 1, BMAX, NPMAX) == (iota(GROUP * NPMAX, wide, 0) & 15),
                            1.0, 0.0)
    fold_slot = iota(wide, FOLD, 1) - BMAX * group_of(wide, FOLD, 1, BMAX, K)
    fold_from = iota(wide, FOLD, 0) - BMAX * group_of(wide, FOLD, 0, BMAX, NPMAX)
    fold[...] = jnp.where((fold_slot == fold_from) & (iota(wide, FOLD, 1) < K * BMAX), 1.0, 0.0).astype(BF16)
    for copy in count_copies:
        copy.wait_recv()
    blocks.wait()
    here = basis_ref[...].astype(F32)
    prev, post = counts[0].astype(F32), counts[1].astype(F32)
    lower = jnp.where(iota(atoms, atoms, 0) < iota(atoms, atoms, 1), 1.0, 0.0).astype(BF16)
    table = jnp.concatenate([prev, here, post, jnp.zeros((5, atoms), F32)], axis=0).astype(BF16)
    first = jnp.dot(table, lower, preferred_element_type=F32).astype(jnp.int32)
    first_ref[...] = jnp.clip(first + (HALO - rows) + rows * iota(8, atoms, 0), 0, rows + 2 * HALO)
    begin_copy = pltpu.make_async_copy(first_ref, starts, start_sem)
    begin_copy.start()
    lines = []
    at = iota(1, atoms, 1)
    for k in range(K):
        d = k - RIM
        near = here
        if d != 0:
            turn = (-d) % atoms
            inside = (at + d >= 0) & (at + d < atoms)
            near = jnp.where(inside, pltpu.roll(here, turn, 1), pltpu.roll(prev if d < 0 else post, turn, 1))
        lines.append(jnp.where(present_ref[k:k + 1, :] > 0, near, 0.0))
    lines.append(proj_ref[...].astype(F32))
    lines.append(jnp.zeros((atoms - K - 1, atoms), F32))
    limit[...] = jnp.concatenate(lines, axis=0).T

    lane = iota(GROUP, FOLD, 1)
    in_k = group_of(GROUP, FOLD, 1, BMAX, K)
    slot = (lane - BMAX * in_k).astype(F32)

    def band_step(t, carry):
        chunk = pl.ds(pl.multiple_of(t * GROUP, GROUP), GROUP)
        bounds = limit[chunk, :]
        reach = jnp.zeros((GROUP, FOLD), F32)
        for k in range(K):
            reach = jnp.where(in_k == k, bounds[:, k:k + 1], reach)
        kept = jnp.where(slot < reach, 1.0, 0.0)
        kept = jnp.broadcast_to(kept[:, None, :], (GROUP, NPMAX, FOLD)).reshape(GROUP * NPMAX, FOLD)
        most = jnp.broadcast_to(bounds[:, K:K + 1], (GROUP, FOLD))
        most = jnp.broadcast_to(most[:, None, :], (GROUP, NPMAX, FOLD)).reshape(GROUP * NPMAX, FOLD)
        valid = (kept > 0.5) & ((iota(GROUP * NPMAX, FOLD, 0) & 15).astype(F32) < most)
        which_k = group_of(GROUP * NPMAX, FOLD, 1, BMAX, K)
        acc = jnp.zeros((GROUP * NPMAX, FOLD), F32)
        for k in range(K):
            block = cm_ref[k, chunk, :].astype(F32)
            block = jnp.broadcast_to(block[:, None, :], (GROUP, NPMAX, wide)).reshape(GROUP * NPMAX, wide)
            folded = jnp.dot((block * spread[...]).astype(BF16), fold[...], preferred_element_type=F32)
            acc = jnp.where(which_k == k, folded, acc)
        acc = jnp.where(valid, acc, 0.0)
        acc = jnp.concatenate([acc, jnp.zeros((acc.shape[0], WIN - FOLD), F32)], axis=1)
        pieces = []
        for a in range(GROUP):
            piece = acc[a * NPMAX:(a + 1) * NPMAX]
            pieces.append(piece if a == 0 else pltpu.roll(piece, a * BMAX, 1))
        band[t] = jnp.concatenate(pieces, axis=0).astype(BF16)
        return carry

    lax.fori_loop(0, atoms // GROUP, band_step, 0)

    for which in (0, 1):
        total = part[which, spot].astype(F32)
        for step in range(1, p):
            plane_copy(which, step).wait_recv()
            total = total + got[which, step].astype(F32)
        middle[which] = total.astype(BF16)
        for step in range(1, q):
            line_copy(which, step).start()

    begin_copy.wait()
    for copy in halos:
        copy.wait()
    length = ext.shape[1]
    lanes = [slice(c * 128, (c + 1) * 128) for c in range(ext.shape[0])]
    chunk_rows = rows // 8

    def widen(t, carry):
        at = pl.multiple_of(t * chunk_rows, 16)
        block = vec[pl.ds(at, chunk_rows), :].astype(F32)
        for c, span in enumerate(lanes):
            ext[c, pl.ds(HALO + at, chunk_rows), :] = block[:, span]
        return carry

    lax.fori_loop(0, 8, widen, 0)
    for side, at in ((0, 0), (1, HALO + rows)):
        block = halo_ref[side].astype(F32)
        for c, span in enumerate(lanes):
            ext[c, at:at + HALO, :] = block[:, span]
    spare = length - 2 * HALO - rows
    ext[:, length - spare:, :] = jnp.zeros((ext.shape[0], spare, 128), F32)
    for which in (0, 1):
        pext[which, 0:length - spare, :] = pan_ref[which].astype(F32)
    pext[:, length - spare:, :] = jnp.zeros((2, spare, half), F32)
    used = (atoms + 2 * RIM) * BMAX
    padded[used:, :] = jnp.zeros((padded.shape[0] - used, padded.shape[1]), BF16)
    ppadded[used:, :] = jnp.zeros((ppadded.shape[0] - used, ppadded.shape[1]), BF16)

    mine = pl.ds(pl.multiple_of(row * slab, slab), slab)
    sums = []
    for which in (0, 1):
        total = middle[which, pl.ds(pl.multiple_of(line * slab, slab), slab), :].astype(F32)
        for step in range(1, q):
            line_copy(which, step).wait_recv()
            total = total + got_line[which, step].astype(F32)
        sums.append(total)
    inner = jnp.concatenate(sums, axis=1)
    mixed = jnp.dot(inner, factor_ref[...], precision=lax.Precision.HIGHEST, preferred_element_type=F32)
    mix_ref[mine, :] = mixed.astype(BF16)

    def mix_copy(step):
        return remote(mix_ref.at[mine], mix_ref.at[mine], mix_sems, (step,), (line_peer(step), col))

    def pass_copy(z, step):
        at = pl.multiple_of((lax.rem(line + q - z, q) * p + spot) * slab, slab)
        return remote(mix_ref.at[pl.ds(at, slab)], mix_ref.at[pl.ds(at, slab)], pass_sems, (z, step),
                      (plane_peer(step), col))

    for step in range(1, q):
        mix_copy(step).start()
    for step in range(1, p):
        pass_copy(0, step).start()

    def gather(t, carry):
        at = pl.multiple_of(2 * t * BMAX, 16)
        begins = []
        for e in (0, 1):
            flat = 2 * t + e + atoms - RIM
            begins.append(starts[lax.div(flat, atoms), lax.rem(flat, atoms)])
        for c, span in enumerate(lanes):
            both = [ext[c, pl.ds(begin, BMAX), :] for begin in begins]
            padded[pl.ds(at, 2 * BMAX), span] = jnp.concatenate(both, axis=0).astype(BF16)
        for c in (0, 1):
            both = [pext[c, pl.ds(begin, BMAX), :] for begin in begins]
            ppadded[pl.ds(at, 2 * BMAX), c * half:(c + 1) * half] = jnp.concatenate(both, axis=0).astype(BF16)
        return carry

    lax.fori_loop(0, (atoms + 2 * RIM) // 2, gather, 0)

    for z in range(1, q):
        mix_copy(z).wait_recv()
        for step in range(1, p):
            pass_copy(z, step).start()

    def project(g, carry):
        at = pl.ds(pl.multiple_of(g * GROUP * BMAX, 16), WIN)
        base_ref[g] = jnp.dot(band[g], padded[at, :], preferred_element_type=F32)
        lean_ref[g] = jnp.dot(band[g], ppadded[at, :], preferred_element_type=F32).astype(BF16)
        return carry

    lax.fori_loop(0, atoms // GROUP, project, 0)
    swap.wait_send()
    for copy in count_copies:
        copy.wait_send()
    for which in (0, 1):
        for step in range(1, p):
            plane_copy(which, step).wait_send()
        for step in range(1, q):
            line_copy(which, step).wait_send()
    for step in range(1, q):
        mix_copy(step).wait_send()
    for z in range(q):
        for step in range(1, p):
            pass_copy(z, step).wait()


def density_kernel(vin_ref, pan_ref, mix_ref, base_ref, lean_ref, mask_ref, occ_ref,
                   vec_ref, den_ref, mixing, weight, *, column_total):
    step = pl.program_id(0)
    tile = vin_ref.shape[0]

    @pl.when(step == 0)
    def _():
        mixing[...] = mix_ref[...].T
        weight[...] = mask_ref[...].astype(F32) * occ_ref[...] / column_total

    at = pl.ds(pl.multiple_of(HALO + step * tile, 16), tile)
    panel = jnp.concatenate([pan_ref[0, at, :], pan_ref[1, at, :]], axis=1)
    update = jnp.dot(panel, mixing[...], preferred_element_type=F32)
    vec_ref[...] = (vin_ref[...].astype(F32) - update).astype(BF16)
    update = jnp.dot(lean_ref[step], mixing[...], preferred_element_type=F32)
    rounded = (base_ref[step] - update).astype(BF16)
    weighted = (rounded.astype(F32) * weight[...]).astype(BF16)
    full = lax.dot_general(weighted, rounded, (((1,), (1,)), ((), ())), preferred_element_type=F32)
    shape = full.shape
    full = jnp.where(iota(*shape, 0) >> 4 == iota(*shape, 1) >> 4, full, 0.0)
    expand = jnp.where((iota(shape[1], NPMAX * NPMAX, 0) & 15) == (iota(shape[1], NPMAX * NPMAX, 1) & 15),
                       1.0, 0.0).astype(BF16)
    spreads = 0.0
    for _ in range(3):
        top = full.astype(BF16)
        spreads = spreads + jnp.dot(top, expand, preferred_element_type=F32)
        full = full - top.astype(F32)
    shape = spreads.shape
    spreads = jnp.where((iota(*shape, 0) & 15) == iota(*shape, 1) >> 4, spreads, 0.0)
    den_ref[...] = spreads.reshape(GROUP, NPMAX, shape[1]).sum(axis=1)


def local(vectors_in, panel, factor, atom_basis, proj_count, coupling, block_present, occ_mask, occ_weight):
    n = lax.axis_size("row")
    rows, cols = vectors_in.shape
    half = panel.shape[1]
    npan = factor.shape[0]
    atoms = atom_basis.shape[1]
    groups = atoms // GROUP
    vmem = pl.BlockSpec(memory_space=pltpu.VMEM)
    hbm = pl.BlockSpec(memory_space=pl.ANY)
    slab = cols // n
    plane = max(d for d in range(1, n + 1) if n % d == 0 and d * d <= n)
    ext_rows = rows + 2 * HALO
    pad_rows = (groups - 1) * GROUP * BMAX + WIN
    dma = pltpu.SemaphoreType.DMA
    operands = (vectors_in, panel, jnp.swapaxes(coupling, 0, 1), factor, atom_basis, proj_count[None, :], block_present.T)
    operands = [pltpu.with_memory_space_constraint(x, pltpu.HBM) for x in operands]
    mix, pan, base, lean = pl.pallas_call(
        functools.partial(mix_kernel, n, plane),
        out_shape=(
            jax.ShapeDtypeStruct((cols, npan), BF16),
            jax.ShapeDtypeStruct((2, ext_rows, half), BF16),
            jax.ShapeDtypeStruct((groups, GROUP * NPMAX, cols), F32),
            jax.ShapeDtypeStruct((groups, GROUP * NPMAX, npan), BF16),
        ),
        in_specs=[hbm] * 3 + [vmem] * 4,
        out_specs=(vmem,) * 4,
        scratch_shapes=[
            pltpu.VMEM((rows, cols), BF16),
            pltpu.VMEM((2, plane, cols // plane, half), BF16),
            pltpu.VMEM((2, plane, cols // plane, half), BF16),
            pltpu.VMEM((2, cols // plane, half), BF16),
            pltpu.VMEM((2, n // plane, slab, half), BF16),
            pltpu.VMEM((2, 1, atoms), jnp.int32),
            pltpu.VMEM((atoms, atoms), F32),
            pltpu.VMEM((GROUP * NPMAX, NPMAX * BMAX), F32),
            pltpu.VMEM((NPMAX * BMAX, FOLD), BF16),
            pltpu.VMEM((K, atoms, NPMAX * BMAX), BF16),
            pltpu.VMEM((2, HALO, cols), BF16),
            pltpu.VMEM((groups, GROUP * NPMAX, WIN), BF16),
            pltpu.VMEM((8, atoms), jnp.int32),
            pltpu.SMEM((8, atoms), jnp.int32),
            pltpu.VMEM((cols // 128, ext_rows + BMAX, 128), F32),
            pltpu.VMEM((2, ext_rows + BMAX, half), F32),
            pltpu.VMEM((pad_rows, cols), BF16),
            pltpu.VMEM((pad_rows, npan), BF16),
            dma, dma, dma, dma, dma((2, 5)), dma((2, 2)), dma((2, 2)),
            dma((2, 2, plane)), dma((2, 2, n // plane)), dma((2, n // plane)), dma((2, n // plane, plane)),
        ],
        compiler_params=pltpu.CompilerParams(collective_id=0, has_side_effects=True, vmem_limit_bytes=40 << 20),
        cost_estimate=pl.CostEstimate(flops=8 * 10**9, bytes_accessed=10 << 20, transcendentals=0),
    )(*operands)

    tile = rows // groups
    vectors, partial = pl.pallas_call(
        functools.partial(density_kernel, column_total=cols * lax.axis_size("col")),
        out_shape=(
            jax.ShapeDtypeStruct((rows, cols), BF16),
            jax.ShapeDtypeStruct((atoms, NPMAX * NPMAX), F32),
        ),
        grid=(groups,),
        in_specs=[pl.BlockSpec((tile, cols), lambda s: (s, 0))] + [vmem] * 6,
        out_specs=[
            pl.BlockSpec((tile, cols), lambda s: (s, 0)),
            pl.BlockSpec((GROUP, NPMAX * NPMAX), lambda s: (s, 0)),
        ],
        scratch_shapes=[pltpu.VMEM((npan, cols), BF16), pltpu.VMEM((1, cols), F32)],
        compiler_params=pltpu.CompilerParams(vmem_limit_bytes=16 << 20),
        cost_estimate=pl.CostEstimate(flops=6 * 10**9, bytes_accessed=10 << 20, transcendentals=0),
    )(operands[0], pan, mix, base, lean, occ_mask[None, :], occ_weight[None, :])

    ncol = lax.axis_size("col")
    share = atoms // ncol
    col = lax.axis_index("col")
    density = lax.dynamic_slice_in_dim(partial, col * share, share, 0)
    for step in range(1, ncol):
        sent = lax.dynamic_slice_in_dim(partial, lax.rem(col + step, ncol) * share, share, 0)
        density = density + lax.ppermute(sent, "col", [(i, (i + step) % ncol) for i in range(ncol)])
    return (vectors, density)


def solution(mesh):
    placed = (
        P("row", "col"),
        P("row", "col"),
        P(),
        P("row", None),
        P("row"),
        P("row", None, None),
        P("row", None),
        P("col"),
        P("col"),
    )
    return jax.shard_map(
        local,
        mesh=mesh,
        in_specs=placed,
        out_specs=(P("row", "col"), P(("row", "col"), None)),
        check_vma=False,
    )
```

```python
import functools

import jax
import jax.numpy as jnp
from jax import lax
from jax.experimental import pallas as pl
from jax.experimental.pallas import tpu as pltpu
from jax.sharding import PartitionSpec as P

NPMAX = 16
BMAX = 24
K = 9
RIM = (K - 1) // 2
HALO = RIM * BMAX
GROUP = 16
WIN = -(-(GROUP + K - 1) * BMAX // 128) * 128
FOLD = -(-K * BMAX // 128) * 128
F32 = jnp.float32
BF16 = jnp.bfloat16
MESH = pl.DeviceIdType.MESH


def iota(rows, columns, axis):
    return lax.broadcasted_iota(jnp.int32, (rows, columns), axis)


def group_of(rows, columns, axis, size, most):
    small = (8, columns) if axis == 1 else (rows, 128)
    index = iota(*small, axis)
    group = jnp.zeros(small, jnp.int32)
    for edge in range(1, most):
        group = group + jnp.where(index >= edge * size, 1, 0)
    return jnp.tile(group, (rows // small[0], columns // small[1]))


def mix_kernel(n, plane, vec_hbm, panel_hbm, coupling_hbm, factor_ref, basis_ref, proj_ref, present_ref,
               mix_ref, pan_ref, base_ref, lean_ref,
               vec, part, got, middle, got_line, counts, limit, spread, fold, cm_ref, halo_ref, band, first_ref, starts,
               ext, pext, padded, ppadded,
               load_sem, own_sem, cm_sem, start_sem, pan_sems, halo_sems, count_sems, plane_sems, line_sems, mix_sems, pass_sems):
    row, col = lax.axis_index("row"), lax.axis_index("col")
    other = 1 - col
    up, down = lax.rem(row + 1, n), lax.rem(row + n - 1, n)
    rows, half = panel_hbm.shape
    slab = mix_ref.shape[0] // n
    body = pl.ds(HALO, rows)
    q, p = n // plane, plane
    line, spot = lax.div(row, p), lax.rem(row, p)

    def plane_peer(step):
        return line * p + lax.rem(spot + step, p)

    def line_peer(step):
        return lax.rem(line + step, q) * p + spot


    own = pltpu.make_async_copy(panel_hbm, pan_ref.at[col, body], own_sem)
    own.start()
    early = pl.ds(0, rows // 2)
    late = pl.ds(rows // 2, rows // 2)
    loads = [pltpu.make_async_copy(vec_hbm.at[part_rows], vec.at[part_rows], load_sem.at[i])
             for i, part_rows in enumerate((early, late))]
    for load in loads:
        load.start()
    blocks = pltpu.make_async_copy(coupling_hbm, cm_ref, cm_sem)
    blocks.start()

    barrier = pltpu.get_barrier_semaphore()
    greeted = [(plane_peer(step), col) for step in range(1, p)] + [(line_peer(step), col) for step in range(1, q)]
    greeted += [(up, col), (down, col)] + [(peer, other) for peer in (row, up, down)]
    for target in greeted:
        pl.semaphore_signal(barrier, inc=1, device_id=target, device_id_type=MESH)
    atoms, wide = cm_ref.shape[1:]
    spread[...] = jnp.where(group_of(GROUP * NPMAX, wide, 1, BMAX, NPMAX) == (iota(GROUP * NPMAX, wide, 0) & 15),
                            1.0, 0.0)
    fold_slot = iota(wide, FOLD, 1) - BMAX * group_of(wide, FOLD, 1, BMAX, K)
    fold_from = iota(wide, FOLD, 0) - BMAX * group_of(wide, FOLD, 0, BMAX, NPMAX)
    fold[...] = jnp.where((fold_slot == fold_from) & (iota(wide, FOLD, 1) < K * BMAX), 1.0, 0.0).astype(BF16)
    own.wait()
    loads[0].wait()
    ahead = lax.dot_general(pan_ref[col, HALO:HALO + rows // 2, :], vec[early, :], (((0,), (0,)), ((), ())),
                            preferred_element_type=F32)
    pl.semaphore_wait(barrier, len(greeted))

    def remote(src, dst, sems, slot, target):
        return pltpu.make_async_remote_copy(
            src_ref=src, dst_ref=dst, send_sem=sems.at[(0,) + slot], recv_sem=sems.at[(1,) + slot],
            device_id=target, device_id_type=MESH)

    swap = remote(panel_hbm, pan_ref.at[col, pl.ds(HALO, rows)], pan_sems, (0,), (row, other))
    swap.start()
    count_copies = [
        remote(basis_ref, counts.at[side], count_sems, (side,), (target, col))
        for side, target in ((0, up), (1, down))
    ]
    for copy in count_copies:
        copy.start()
    halos = []
    for side, target in ((0, up), (1, down)):
        src_at = rows - HALO if side == 0 else 0
        dst_at = 0 if side == 0 else HALO + rows
        for where in (0, 1):
            to = col if where == 0 else other
            halos.append(remote(panel_hbm.at[pl.ds(src_at, HALO)], pan_ref.at[col, pl.ds(dst_at, HALO)],
                                pan_sems, (1 + 2 * side + where,), (target, to)))
        halos.append(remote(vec_hbm.at[pl.ds(src_at, HALO)], halo_ref.at[side], halo_sems, (side,), (target, col)))
    loads[1].wait()

    def product(which, piece):
        piece = piece.T.astype(BF16)
        for z in range(q):
            for at in range(p):
                part[which, at, z * slab:(z + 1) * slab] = piece[(z * p + at) * slab:(z * p + at + 1) * slab]

    def plane_copy(which, step):
        return remote(part.at[which, lax.rem(spot + step, p)], got.at[which, step], plane_sems, (which, step),
                      (plane_peer(step), col))

    def line_copy(which, step):
        at = pl.multiple_of(lax.rem(line + step, q) * slab, slab)
        return remote(middle.at[which, pl.ds(at, slab)], got_line.at[which, step], line_sems, (which, step),
                      (line_peer(step), col))

    contract = (((0,), (0,)), ((), ()))
    product(col, ahead + lax.dot_general(pan_ref[col, HALO + rows // 2:HALO + rows, :], vec[late, :], contract,
                                         preferred_element_type=F32))
    for step in range(1, p):
        plane_copy(col, step).start()
    swap.wait_recv()
    product(other, lax.dot_general(pan_ref[other, HALO:HALO + rows, :], vec[...], contract,
                                   preferred_element_type=F32))
    for step in range(1, p):
        plane_copy(other, step).start()
    for copy in halos:
        copy.start()

    for copy in count_copies:
        copy.wait_recv()
    blocks.wait()
    here = basis_ref[...].astype(F32)
    prev, post = counts[0].astype(F32), counts[1].astype(F32)
    lower = jnp.where(iota(atoms, atoms, 0) < iota(atoms, atoms, 1), 1.0, 0.0).astype(BF16)
    table = jnp.concatenate([prev, here, post, jnp.zeros((5, atoms), F32)], axis=0).astype(BF16)
    first = jnp.dot(table, lower, preferred_element_type=F32).astype(jnp.int32)
    first_ref[...] = jnp.clip(first + (HALO - rows) + rows * iota(8, atoms, 0), 0, rows + 2 * HALO)
    begin_copy = pltpu.make_async_copy(first_ref, starts, start_sem)
    begin_copy.start()
    lines = []
    at = iota(1, atoms, 1)
    for k in range(K):
        d = k - RIM
        near = here
        if d != 0:
            turn = (-d) % atoms
            inside = (at + d >= 0) & (at + d < atoms)
            near = jnp.where(inside, pltpu.roll(here, turn, 1), pltpu.roll(prev if d < 0 else post, turn, 1))
        lines.append(jnp.where(present_ref[k:k + 1, :] > 0, near, 0.0))
    lines.append(proj_ref[...].astype(F32))
    lines.append(jnp.zeros((atoms - K - 1, atoms), F32))
    limit[...] = jnp.concatenate(lines, axis=0).T

    lane = iota(GROUP, FOLD, 1)
    in_k = group_of(GROUP, FOLD, 1, BMAX, K)
    slot = (lane - BMAX * in_k).astype(F32)

    def band_step(t, carry):
        chunk = pl.ds(pl.multiple_of(t * GROUP, GROUP), GROUP)
        bounds = limit[chunk, :]
        reach = jnp.zeros((GROUP, FOLD), F32)
        for k in range(K):
            reach = jnp.where(in_k == k, bounds[:, k:k + 1], reach)
        kept = jnp.where(slot < reach, 1.0, 0.0)
        kept = jnp.broadcast_to(kept[:, None, :], (GROUP, NPMAX, FOLD)).reshape(GROUP * NPMAX, FOLD)
        most = jnp.broadcast_to(bounds[:, K:K + 1], (GROUP, FOLD))
        most = jnp.broadcast_to(most[:, None, :], (GROUP, NPMAX, FOLD)).reshape(GROUP * NPMAX, FOLD)
        valid = (kept > 0.5) & ((iota(GROUP * NPMAX, FOLD, 0) & 15).astype(F32) < most)
        which_k = group_of(GROUP * NPMAX, FOLD, 1, BMAX, K)
        acc = jnp.zeros((GROUP * NPMAX, FOLD), F32)
        for k in range(K):
            block = cm_ref[k, chunk, :].astype(F32)
            block = jnp.broadcast_to(block[:, None, :], (GROUP, NPMAX, wide)).reshape(GROUP * NPMAX, wide)
            folded = jnp.dot((block * spread[...]).astype(BF16), fold[...], preferred_element_type=F32)
            acc = jnp.where(which_k == k, folded, acc)
        acc = jnp.where(valid, acc, 0.0)
        acc = jnp.concatenate([acc, jnp.zeros((acc.shape[0], WIN - FOLD), F32)], axis=1)
        pieces = []
        for a in range(GROUP):
            piece = acc[a * NPMAX:(a + 1) * NPMAX]
            pieces.append(piece if a == 0 else pltpu.roll(piece, a * BMAX, 1))
        band[t] = jnp.concatenate(pieces, axis=0).astype(BF16)
        return carry

    lax.fori_loop(0, atoms // GROUP, band_step, 0)

    for which in (0, 1):
        total = part[which, spot].astype(F32)
        for step in range(1, p):
            plane_copy(which, step).wait_recv()
            total = total + got[which, step].astype(F32)
        middle[which] = total.astype(BF16)
        for step in range(1, q):
            line_copy(which, step).start()

    begin_copy.wait()
    for copy in halos:
        copy.wait()
    length = ext.shape[1]
    lanes = [slice(c * 128, (c + 1) * 128) for c in range(ext.shape[0])]
    chunk_rows = rows // 8

    def widen(t, carry):
        at = pl.multiple_of(t * chunk_rows, 16)
        block = vec[pl.ds(at, chunk_rows), :].astype(F32)
        for c, span in enumerate(lanes):
            ext[c, pl.ds(HALO + at, chunk_rows), :] = block[:, span]
        return carry

    lax.fori_loop(0, 8, widen, 0)
    for side, at in ((0, 0), (1, HALO + rows)):
        block = halo_ref[side].astype(F32)
        for c, span in enumerate(lanes):
            ext[c, at:at + HALO, :] = block[:, span]
    spare = length - 2 * HALO - rows
    ext[:, length - spare:, :] = jnp.zeros((ext.shape[0], spare, 128), F32)
    for which in (0, 1):
        pext[which, 0:length - spare, :] = pan_ref[which].astype(F32)
    pext[:, length - spare:, :] = jnp.zeros((2, spare, half), F32)
    used = (atoms + 2 * RIM) * BMAX
    padded[used:, :] = jnp.zeros((padded.shape[0] - used, padded.shape[1]), BF16)
    ppadded[used:, :] = jnp.zeros((ppadded.shape[0] - used, ppadded.shape[1]), BF16)

    mine = pl.ds(pl.multiple_of(row * slab, slab), slab)
    sums = []
    for which in (0, 1):
        total = middle[which, pl.ds(pl.multiple_of(line * slab, slab), slab), :].astype(F32)
        for step in range(1, q):
            line_copy(which, step).wait_recv()
            total = total + got_line[which, step].astype(F32)
        sums.append(total)
    inner = jnp.concatenate(sums, axis=1)
    mixed = jnp.dot(inner, factor_ref[...], precision=lax.Precision.HIGHEST, preferred_element_type=F32)
    mix_ref[mine, :] = mixed.astype(BF16)

    def mix_copy(step):
        return remote(mix_ref.at[mine], mix_ref.at[mine], mix_sems, (step,), (line_peer(step), col))

    def pass_copy(z, step):
        at = pl.multiple_of((lax.rem(line + q - z, q) * p + spot) * slab, slab)
        return remote(mix_ref.at[pl.ds(at, slab)], mix_ref.at[pl.ds(at, slab)], pass_sems, (z, step),
                      (plane_peer(step), col))

    for step in range(1, q):
        mix_copy(step).start()
    for step in range(1, p):
        pass_copy(0, step).start()

    def gather(t, carry):
        at = pl.multiple_of(2 * t * BMAX, 16)
        begins = []
        for e in (0, 1):
            flat = 2 * t + e + atoms - RIM
            begins.append(starts[lax.div(flat, atoms), lax.rem(flat, atoms)])
        for c, span in enumerate(lanes):
            both = [ext[c, pl.ds(begin, BMAX), :] for begin in begins]
            padded[pl.ds(at, 2 * BMAX), span] = jnp.concatenate(both, axis=0).astype(BF16)
        for c in (0, 1):
            both = [pext[c, pl.ds(begin, BMAX), :] for begin in begins]
            ppadded[pl.ds(at, 2 * BMAX), c * half:(c + 1) * half] = jnp.concatenate(both, axis=0).astype(BF16)
        return carry

    lax.fori_loop(0, (atoms + 2 * RIM) // 2, gather, 0)

    for z in range(1, q):
        mix_copy(z).wait_recv()
        for step in range(1, p):
            pass_copy(z, step).start()

    def project(g, carry):
        at = pl.ds(pl.multiple_of(g * GROUP * BMAX, 16), WIN)
        base_ref[g] = jnp.dot(band[g], padded[at, :], preferred_element_type=F32)
        lean_ref[g] = jnp.dot(band[g], ppadded[at, :], preferred_element_type=F32).astype(BF16)
        return carry

    lax.fori_loop(0, atoms // GROUP, project, 0)
    swap.wait_send()
    for copy in count_copies:
        copy.wait_send()
    for which in (0, 1):
        for step in range(1, p):
            plane_copy(which, step).wait_send()
        for step in range(1, q):
            line_copy(which, step).wait_send()
    for step in range(1, q):
        mix_copy(step).wait_send()
    for z in range(q):
        for step in range(1, p):
            pass_copy(z, step).wait()


def density_kernel(vin_ref, pan_ref, mix_ref, base_ref, lean_ref, mask_ref, occ_ref,
                   vec_ref, den_ref, mixing, weight, *, column_total):
    step = pl.program_id(0)
    tile = vin_ref.shape[0]

    @pl.when(step == 0)
    def _():
        mixing[...] = mix_ref[...].T
        weight[...] = mask_ref[...].astype(F32) * occ_ref[...] / column_total

    at = pl.ds(pl.multiple_of(HALO + step * tile, 16), tile)
    panel = jnp.concatenate([pan_ref[0, at, :], pan_ref[1, at, :]], axis=1)
    update = jnp.dot(panel, mixing[...], preferred_element_type=F32)
    vec_ref[...] = (vin_ref[...].astype(F32) - update).astype(BF16)
    update = jnp.dot(lean_ref[step], mixing[...], preferred_element_type=F32)
    rounded = (base_ref[step] - update).astype(BF16)
    weighted = (rounded.astype(F32) * weight[...]).astype(BF16)
    full = lax.dot_general(weighted, rounded, (((1,), (1,)), ((), ())), preferred_element_type=F32)
    shape = full.shape
    full = jnp.where(iota(*shape, 0) >> 4 == iota(*shape, 1) >> 4, full, 0.0)
    expand = jnp.where((iota(shape[1], NPMAX * NPMAX, 0) & 15) == (iota(shape[1], NPMAX * NPMAX, 1) & 15),
                       1.0, 0.0).astype(BF16)
    spreads = 0.0
    for _ in range(3):
        top = full.astype(BF16)
        spreads = spreads + jnp.dot(top, expand, preferred_element_type=F32)
        full = full - top.astype(F32)
    shape = spreads.shape
    spreads = jnp.where((iota(*shape, 0) & 15) == iota(*shape, 1) >> 4, spreads, 0.0)
    den_ref[...] = spreads.reshape(GROUP, NPMAX, shape[1]).sum(axis=1)


def local(vectors_in, panel, factor, atom_basis, proj_count, coupling, block_present, occ_mask, occ_weight):
    n = lax.axis_size("row")
    rows, cols = vectors_in.shape
    half = panel.shape[1]
    npan = factor.shape[0]
    atoms = atom_basis.shape[1]
    groups = atoms // GROUP
    vmem = pl.BlockSpec(memory_space=pltpu.VMEM)
    hbm = pl.BlockSpec(memory_space=pl.ANY)
    slab = cols // n
    plane = max(d for d in range(1, n + 1) if n % d == 0 and d * d <= n)
    ext_rows = rows + 2 * HALO
    pad_rows = (groups - 1) * GROUP * BMAX + WIN
    dma = pltpu.SemaphoreType.DMA
    operands = (vectors_in, panel, jnp.swapaxes(coupling, 0, 1), factor, atom_basis, proj_count[None, :], block_present.T)
    operands = [pltpu.with_memory_space_constraint(x, pltpu.HBM) for x in operands]
    mix, pan, base, lean = pl.pallas_call(
        functools.partial(mix_kernel, n, plane),
        out_shape=(
            jax.ShapeDtypeStruct((cols, npan), BF16),
            jax.ShapeDtypeStruct((2, ext_rows, half), BF16),
            jax.ShapeDtypeStruct((groups, GROUP * NPMAX, cols), F32),
            jax.ShapeDtypeStruct((groups, GROUP * NPMAX, npan), BF16),
        ),
        in_specs=[hbm] * 3 + [vmem] * 4,
        out_specs=(vmem,) * 4,
        scratch_shapes=[
            pltpu.VMEM((rows, cols), BF16),
            pltpu.VMEM((2, plane, cols // plane, half), BF16),
            pltpu.VMEM((2, plane, cols // plane, half), BF16),
            pltpu.VMEM((2, cols // plane, half), BF16),
            pltpu.VMEM((2, n // plane, slab, half), BF16),
            pltpu.VMEM((2, 1, atoms), jnp.int32),
            pltpu.VMEM((atoms, atoms), F32),
            pltpu.VMEM((GROUP * NPMAX, NPMAX * BMAX), F32),
            pltpu.VMEM((NPMAX * BMAX, FOLD), BF16),
            pltpu.VMEM((K, atoms, NPMAX * BMAX), BF16),
            pltpu.VMEM((2, HALO, cols), BF16),
            pltpu.VMEM((groups, GROUP * NPMAX, WIN), BF16),
            pltpu.VMEM((8, atoms), jnp.int32),
            pltpu.SMEM((8, atoms), jnp.int32),
            pltpu.VMEM((cols // 128, ext_rows + BMAX, 128), F32),
            pltpu.VMEM((2, ext_rows + BMAX, half), F32),
            pltpu.VMEM((pad_rows, cols), BF16),
            pltpu.VMEM((pad_rows, npan), BF16),
            dma((2,)), dma, dma, dma, dma((2, 5)), dma((2, 2)), dma((2, 2)),
            dma((2, 2, plane)), dma((2, 2, n // plane)), dma((2, n // plane)), dma((2, n // plane, plane)),
        ],
        compiler_params=pltpu.CompilerParams(collective_id=0, has_side_effects=True, vmem_limit_bytes=40 << 20),
        cost_estimate=pl.CostEstimate(flops=8 * 10**9, bytes_accessed=10 << 20, transcendentals=0),
    )(*operands)

    tile = rows // groups
    vectors, partial = pl.pallas_call(
        functools.partial(density_kernel, column_total=cols * lax.axis_size("col")),
        out_shape=(
            jax.ShapeDtypeStruct((rows, cols), BF16),
            jax.ShapeDtypeStruct((atoms, NPMAX * NPMAX), F32),
        ),
        grid=(groups,),
        in_specs=[pl.BlockSpec((tile, cols), lambda s: (s, 0))] + [vmem] * 6,
        out_specs=[
            pl.BlockSpec((tile, cols), lambda s: (s, 0)),
            pl.BlockSpec((GROUP, NPMAX * NPMAX), lambda s: (s, 0)),
        ],
        scratch_shapes=[pltpu.VMEM((npan, cols), BF16), pltpu.VMEM((1, cols), F32)],
        compiler_params=pltpu.CompilerParams(vmem_limit_bytes=16 << 20),
        cost_estimate=pl.CostEstimate(flops=6 * 10**9, bytes_accessed=10 << 20, transcendentals=0),
    )(operands[0], pan, mix, base, lean, occ_mask[None, :], occ_weight[None, :])

    ncol = lax.axis_size("col")
    share = atoms // ncol
    col = lax.axis_index("col")
    density = lax.dynamic_slice_in_dim(partial, col * share, share, 0)
    for step in range(1, ncol):
        sent = lax.dynamic_slice_in_dim(partial, lax.rem(col + step, ncol) * share, share, 0)
        density = density + lax.ppermute(sent, "col", [(i, (i + step) % ncol) for i in range(ncol)])
    return (vectors, density)


def solution(mesh):
    placed = (
        P("row", "col"),
        P("row", "col"),
        P(),
        P("row", None),
        P("row"),
        P("row", None, None),
        P("row", None),
        P("col"),
        P("col"),
    )
    return jax.shard_map(
        local,
        mesh=mesh,
        in_specs=placed,
        out_specs=(P("row", "col"), P(("row", "col"), None)),
        check_vma=False,
    )
```
